32 devices in a mesh: chan: 4 (over y, x), slab: 8 (over z, core).
Axes of the slice: x: 2, y: 2, z: 4, core: 2. Of those that a mesh axis runs over, the one named last changes fastest.
Arguments:
- volume: bfloat16 [128, 16, 128, 128], P('chan', 'slab'), may hold values from -6 to 6
- weight_one: bfloat16 [3, 3, 3, 128, 256], P(None, None, None, 'chan'), may hold values from -0.125 to 0.125
- bias_one: float32 [256], replicated, may hold values from -3 to 3
- weight_two: bfloat16 [3, 3, 3, 32, 256], replicated, may hold values from -0.21875 to 0.21875
- bias_two: float32 [256], replicated, may hold values from -3 to 3
Outputs:
- activated: bfloat16 [8, 64, 64, 256], P('slab', 'chan')
- grouped: bfloat16 [8, 64, 64, 256], P('slab', 'chan')
The draws below stay inside these ranges and needn't reach their ends.
All inputs are finite; a program needn't handle non-finite values.
Results may differ from the reference program's by a relative error of at most 0.018.
Values may be sent and summed in bfloat16 or wider, within the bound.
A program may use at most 64 MiB of HBM per device.

```python
import jax
import jax.numpy as jnp
from jax import lax

CIN = 128
COUT = 256
GROUPS = 8
SIDE = 128
DEPTH = 16
N_CHAN = 4


def raised(values, stream_key, source, target, blocks, factor):
    owner, partner = [(jnp.arange(values.shape[position]) // (values.shape[position] // blocks)).reshape([-1 if axis == position else 1 for axis in range(values.ndim)]) for position in (source, target)]
    chosen = jax.random.permutation(stream_key, blocks)[partner]
    strong = (owner == chosen) | (owner == (partner + blocks // 2) % blocks)
    return jnp.where(strong, factor * values, values)


def levels(stream_key, dims, pieces, low, top_value):
    level, own = 1.0, jax.random.fold_in(stream_key, 6)
    for position, parts in pieces:
        heights = jnp.exp(jax.random.uniform(jax.random.fold_in(own, position), (parts,), jnp.float32, low / len(pieces), top_value / len(pieces)))
        level = level * jnp.repeat(heights, dims[position] // parts).reshape([-1 if axis == position else 1 for axis in range(len(dims))])
    return level


def centred(stream_key, shape, deviation, limit, split=(), dtype=jnp.bfloat16):
    array = deviation * jax.random.normal(stream_key, shape, jnp.float32)
    if split:
        array = array * levels(stream_key, shape, split, -0.22, 0.18)
    return jnp.clip(array, -limit, limit).astype(dtype)


def noise_with(own_key, shape, scale, limit, split, heavy, kind=jnp.bfloat16):
    drawn = scale * jax.random.normal(own_key, shape, jnp.float32)
    if split:
        drawn = drawn * levels(own_key, shape, split, -0.22, 0.18)
    return jnp.clip(raised(drawn, jax.random.fold_in(own_key, 3), *heavy), -limit, limit).astype(kind)


def setup_inputs(seed: int = 0) -> dict:
    arg_keys = jax.random.split(jax.random.key(seed), 6)
    return {
        "volume": centred(arg_keys[0], (CIN, DEPTH, SIDE, SIDE), 1.0, 6.0, ((0, 4), (1, 8))),
        "weight_one": noise_with(arg_keys[1], (3, 3, 3, CIN, COUT), (27 * CIN) ** -0.5, 0.125, ((3, 4),), (3, 4, 4, 2.0)),
        "bias_one": centred(arg_keys[2], (COUT,), 0.5, 3.0, (), jnp.float32),
        "weight_two": centred(arg_keys[3], (3, 3, 3, COUT // GROUPS, COUT), (27 * (COUT // GROUPS)) ** -0.5, 0.21875),
        "bias_two": centred(arg_keys[4], (COUT,), 0.5, 3.0, (), jnp.float32),
    }


def leaky(value):
    return jnp.where(value > 0, value, 0.3 * value)


def reference(volume, weight_one, bias_one, weight_two, bias_two):
    block = CIN // N_CHAN
    blocks = volume.reshape(N_CHAN, block, DEPTH, SIDE, SIDE)
    kernels = weight_one.reshape(3, 3, 3, N_CHAN, block, COUT).transpose(3, 0, 1, 2, 4, 5)

    def add_block(total, pair):
        piece, kernel = pair
        part = lax.conv_general_dilated(
            piece[None].astype(jnp.float32), kernel.astype(jnp.float32), (2, 2, 2),
            ((1, 0), (1, 0), (1, 0)), dimension_numbers=("NCDHW", "DHWIO", "NDHWC"),
            precision=lax.Precision.HIGHEST)[0]
        rounded = lax.optimization_barrier(part.astype(jnp.bfloat16))
        return total + rounded.astype(jnp.float32), None

    start = jnp.zeros((DEPTH // 2, SIDE // 2, SIDE // 2, COUT), jnp.float32)
    summed, _ = lax.scan(add_block, start, (blocks, kernels))
    activated = leaky(summed + bias_one.astype(jnp.float32)).astype(jnp.bfloat16)
    second = lax.conv_general_dilated(
        activated[None].astype(jnp.float32), weight_two.astype(jnp.float32), (1, 1, 1),
        ((1, 1), (1, 1), (1, 1)), dimension_numbers=("NDHWC", "DHWIO", "NDHWC"),
        feature_group_count=GROUPS, precision=lax.Precision.HIGHEST)[0]
    grouped = (second + bias_two.astype(jnp.float32)).astype(jnp.bfloat16)
    return activated, grouped
```

```python
import functools

import jax
import jax.numpy as jnp
from jax import lax
from jax.experimental import pallas as pl
from jax.experimental.pallas import tpu as pltpu
from jax.sharding import PartitionSpec as P

BF = jnp.bfloat16
F32 = jnp.float32
MESH = pl.DeviceIdType.MESH
AROUND = [(0, 1), (0, -1), (1, 0), (-1, 0), (1, 1), (1, -1), (-1, 1), (-1, -1)]


def leaky(value):
    return jnp.where(value > 0, value, 0.3 * value)


def square(slabs, vol_ref, k1_ref, b1_ref, k2_ref, b2_ref, act_ref, out_ref,
           x_ref, low_ref, t_ref, part_ref, recv_ref, a_ref, w1_ref, w2_ref, acc_ref,
           load_sem, low_send, low_recv, sum_send, sum_recv, relay_send, relay_recv,
           halo_send, halo_recv, row_send, row_recv, pass_send, pass_recv):
    parts = 4
    c, _, bands, deep, width = vol_ref.shape
    mine, q, k = act_ref.shape
    half = width // 2
    me, slab = lax.axis_index("chan"), lax.axis_index("slab")
    core = lax.rem(slab, 2)

    def peer(s):
        return 2 * lax.rem(me // 2 + lax.div(s, 2), 2) + lax.rem(lax.rem(me, 2) + lax.rem(s, 2), 2)

    def turn(n):
        return jnp.where(n == 0, 3, jnp.where(n == 3, 0, n))

    far, across_x, across_y = (peer(jnp.int32(s)) for s in (3, 1, 2))
    above, below = slab + 1 < slabs, slab > 0

    def there(ds):
        return above if ds > 0 else below

    barrier = pltpu.get_barrier_semaphore()
    for s in range(1, parts):
        pl.semaphore_signal(barrier, inc=1, device_id={"chan": peer(jnp.int32(s)), "slab": slab}, device_id_type=MESH)
    for ds in (1, -1):
        @pl.when(there(ds))
        def _(ds=ds):
            pl.semaphore_signal(barrier, inc=1, device_id={"chan": me, "slab": slab + ds}, device_id_type=MESH)

    def load(d, n):
        some = pl.ds(n * (bands // 2), bands // 2)
        return pltpu.make_async_copy(vol_ref.at[:, d, some], x_ref.at[d, :, some], load_sem.at[d, n])

    for d in range(2):
        for n in range(2):
            load(d, n).start()

    w1_ref[...] = jnp.zeros_like(w1_ref)
    for e in range(9):
        i, l = divmod(e, 3)
        for par in range(2):
            for j in range(3):
                start = e * 256 + (3 + 2 * par + j) * c
                w1_ref[start:start + c, par * k:(par + 1) * k] = k1_ref[i, j, l]
    size = c * deep
    to, of = (lax.broadcasted_iota(jnp.int32, (size, size), n) for n in range(2))
    perm = jnp.where(of == lax.rem(to, c) * deep + lax.div(to, c), 1.0, 0.0).astype(BF)
    spot = lax.broadcasted_iota(jnp.int32, (half, width), 1) - 2 * lax.broadcasted_iota(jnp.int32, (half, width), 0)
    sel = jnp.concatenate([jnp.where(spot == l - 1, 1.0, 0.0) for l in range(3)], axis=0).astype(BF)
    for e in range(9):
        t_ref[e, 0] = jnp.zeros_like(t_ref[e, 0])

    def decimate(d, pair):
        source = low_ref if d == 0 else x_ref.at[d - 1]
        x = jnp.concatenate([source[:, 2 * pair + v].reshape(size, width) for v in range(2)], axis=1)
        x = jnp.dot(perm, x, preferred_element_type=F32).astype(BF)
        for v in range(2):
            t = lax.dot_general(sel, x[:, v * width:(v + 1) * width], (((1,), (1,)), ((), ())),
                                preferred_element_type=F32).astype(BF)
            for l in range(3):
                for g in range(2):
                    t_ref[3 * d + l, 4 * pair + 2 * v + g + 1] = t[l * half:(l + 1) * half, 128 * g:128 * (g + 1)]

    def plane(d):
        def go(pair, carry):
            decimate(d, pair)
            return carry

        for n in range(2):
            load(d - 1, n).wait()
            lax.fori_loop(n * bands // 4, (n + 1) * bands // 4, go, 0, unroll=UNROLL)

    plane(1)

    @pl.when(jnp.logical_not(below))
    def _():
        low_ref[...] = jnp.zeros_like(low_ref)
        a_ref[0] = jnp.zeros_like(a_ref[0])

    @pl.when(jnp.logical_not(above))
    def _():
        a_ref[2] = jnp.zeros_like(a_ref[2])

    for edge, row in ((0, 0), (parts - 1, mine + 1)):
        @pl.when(me == edge)
        def _(row=row):
            for i in range(3):
                a_ref[i, row] = jnp.zeros_like(a_ref[i, row])

    one = jnp.int32(1)
    across = jnp.minimum(slab, one) + jnp.minimum(jnp.int32(slabs - 1) - slab, one)
    pl.semaphore_wait(barrier, jnp.int32(parts - 1) + across)

    def low_copy(pair):
        some = pl.ds(2 * pair, 2)
        return pltpu.make_async_remote_copy(
            src_ref=vol_ref.at[:, 1, some], dst_ref=low_ref.at[:, some],
            send_sem=low_send.at[pair], recv_sem=low_recv.at[pair],
            device_id={"chan": me, "slab": slab + 1}, device_id_type=MESH)

    def place(r):
        s = 2 * lax.rem(me // 2 + lax.div(r, 2), 2) + lax.rem(lax.rem(me, 2) + lax.rem(r, 2), 2)
        return turn(s)

    def needed(n, act):
        r = peer(turn(n))

        def go(m, carry):
            early = jnp.logical_and(r > 0, place(jnp.maximum(r - 1, 0)) > n)
            late = jnp.logical_or(r == parts - 1, place(jnp.minimum(r + 1, parts - 1)) > n)
            ok = jnp.logical_or(m == 1, jnp.logical_or(jnp.logical_and(m == 0, early), jnp.logical_and(m == 2, late)))

            @pl.when(ok)
            def _():
                act(2 * r + m - 1)
            return carry

        lax.fori_loop(0, 3, go, 0)

    @pl.when(above)
    def _():
        def go(n, carry):
            needed(n, lambda pair: low_copy(pair).start())
            return carry

        lax.fori_loop(0, parts, go, 0)

    plane(2)

    def spread():
        m = k2_ref.shape[3]
        group = lax.broadcasted_iota(jnp.int32, (m, k), 1) // m
        for i in range(3):
            for l in range(3):
                for j in range(3):
                    taps = k2_ref[i, j, l]
                    for g in range(k // m):
                        w2_ref[i, l, j * k + g * m:j * k + (g + 1) * m] = jnp.where(group == g, taps, jnp.zeros_like(taps))

    def first(h, u):
        return 4 * h if u == 0 else 12 - 4 * h

    def chunk(r, h):
        bands4 = [4 * r + h, 4 * r + 3 - h]
        lhs = []
        for e in range(9):
            for lag in range(2):
                lhs.append(jnp.concatenate(
                    [t_ref[e, pl.ds(2 * b + lag, 2)].reshape(2 * half, 128) for b in bands4], axis=0))
        res = jnp.dot(jnp.concatenate(lhs, axis=1), w1_ref[...], preferred_element_type=F32).astype(BF)
        for u, b in enumerate(bands4):
            for v in range(2):
                for par in range(2):
                    at = (2 * u + v) * half
                    part_ref[4 * b + 2 * v + par] = res[at:at + half, par * k:(par + 1) * k]

    def stage(slot, h, u):
        to = peer(jnp.int32(1 + u))
        block = far if slot == 1 else to
        return pltpu.make_async_remote_copy(
            src_ref=part_ref.at[pl.ds(block * mine + first(h, u), 4)], dst_ref=recv_ref.at[slot, pl.ds(first(h, u), 4)],
            send_sem=sum_send.at[slot, h, u], recv_sem=sum_recv.at[slot, h, u],
            device_id={"chan": to, "slab": slab}, device_id_type=MESH)

    def row2(h, u, v):
        return first(h, u) + (2 * v if u == 0 else 2 - 2 * v)

    def relay_copy(h, u, v):
        to = peer(jnp.int32(2 - u))
        at = row2(h, u, v)
        return pltpu.make_async_remote_copy(
            src_ref=part_ref.at[pl.ds(to * mine + at, 2)], dst_ref=recv_ref.at[2, pl.ds(at, 2)],
            send_sem=relay_send.at[h, u, v], recv_sem=relay_recv.at[h, u, v],
            device_id={"chan": to, "slab": slab}, device_id_type=MESH)

    def relay(h):
        for v in range(2):
            for u, block in ((0, across_y), (1, across_x)):
                if v == 0:
                    stage(1, h, u).wait_recv()
                at = row2(h, u, v)
                here = pl.ds(block * mine + at, 2)
                both = part_ref[here].astype(F32) + recv_ref[1, pl.ds(at, 2)].astype(F32)
                part_ref[here] = both.astype(BF)
                relay_copy(h, u, v).start()

    def go(m, carry):
        h, n = lax.div(m, 4), lax.rem(m, 4)

        @pl.when(h == 0)
        def _():
            def take(pair):
                @pl.when(below)
                def _():
                    low_copy(pair).wait_recv()
                decimate(0, pair)

            needed(n, take)

        @pl.when(m == 3)
        def _():
            relay(0)

        chunk(peer(turn(n)), h)

        @pl.when(n == 0)
        def _():
            stage(1, h, 0).start()
            stage(1, h, 1).start()

        @pl.when(n == 1)
        def _():
            stage(0, h, 0).start()

        @pl.when(n == 2)
        def _():
            stage(0, h, 1).start()
        return carry

    lax.fori_loop(0, 8, go, 0)
    relay(1)

    def halo_copy(ds, h, u, v):
        at = pl.ds(row2(h, u, v) + 1, 2)
        n = (1 - ds) // 2
        return pltpu.make_async_remote_copy(
            src_ref=a_ref.at[1, at], dst_ref=a_ref.at[1 - ds, at],
            send_sem=halo_send.at[n, h, u, v], recv_sem=halo_recv.at[n, h, u, v],
            device_id={"chan": me, "slab": slab + ds}, device_id_type=MESH)

    def row_copy(dc):
        n = (1 - dc) // 2
        return pltpu.make_async_remote_copy(
            src_ref=a_ref.at[1, pl.ds(mine if dc > 0 else 1, 1)], dst_ref=a_ref.at[1, pl.ds(0 if dc > 0 else mine + 1, 1)],
            send_sem=row_send.at[n], recv_sem=row_recv.at[n],
            device_id={"chan": me + dc, "slab": slab}, device_id_type=MESH)

    def pass_copy(ds, dc):
        n, e = (1 - ds) // 2, (1 - dc) // 2
        row = pl.ds(0 if dc > 0 else mine + 1, 1)
        return pltpu.make_async_remote_copy(
            src_ref=a_ref.at[1, row], dst_ref=a_ref.at[1 - ds, row],
            send_sem=pass_send.at[n, e], recv_sem=pass_recv.at[n, e],
            device_id={"chan": me, "slab": slab + ds}, device_id_type=MESH)

    def beside(dc):
        return me + 1 < parts if dc > 0 else me > 0

    def activate(h):
        for v in range(2):
            for u in range(2):
                if v == 0:
                    stage(0, h, u).wait_recv()
                relay_copy(h, u, v).wait_recv()
                at = row2(h, u, v)
                total = part_ref[pl.ds(me * mine + at, 2)].astype(F32)
                for slot in (0, 2):
                    total += recv_ref[slot, pl.ds(at, 2)].astype(F32)
                act = leaky(total + b1_ref[...]).astype(BF)
                act_ref[pl.ds(at, 2)] = act
                a_ref[1, pl.ds(at + 1, 2)] = act
                for ds in (1, -1):
                    @pl.when(there(ds))
                    def _(ds=ds, u=u, v=v):
                        halo_copy(ds, h, u, v).start()

    def arrive(ds, late):
        @pl.when(there(-ds))
        def _():
            for h in range(2):
                for v in range(2):
                    if (h == 1 and v == 1) == late:
                        for u in range(2):
                            halo_copy(ds, h, u, v).wait_recv()
            if not late:
                for dc in (1, -1):
                    @pl.when(beside(-dc))
                    def _(dc=dc):
                        pass_copy(ds, dc).wait_recv()

    def convolve(i, lo, hi, fresh, last):
        def rows4(n, carry):
            b = jnp.where(n == 1, 3, jnp.maximum(n - 1, 0))
            lhs = jnp.concatenate([a_ref[i, pl.ds(4 * b + j, 4)].reshape(4 * q, k) for j in range(3)], axis=1)
            here = pl.ds(4 * q * b, 4 * q)
            accs = []
            for l in range(3):
                acc = jnp.dot(lhs, w2_ref[i, l], preferred_element_type=F32)
                if not fresh:
                    acc += acc_ref[l, here]
                accs.append(acc)
            if not last:
                for l in range(3):
                    acc_ref[l, here] = accs[l]
                return carry
            col = lax.rem(lax.broadcasted_iota(jnp.int32, (4 * q, k), 0), q)
            left = jnp.where(col == 0, 0.0, pltpu.roll(accs[0], 1, 0))
            right = jnp.where(col == q - 1, 0.0, pltpu.roll(accs[2], 4 * q - 1, 0))
            res = left + accs[1] + right + b2_ref[...]
            out_ref[pl.ds(4 * b, 4)] = res.reshape(4, q, k).astype(BF)
            return carry

        lax.fori_loop(lo, hi, rows4, 0)

    spread()
    activate(0)
    for dc in (1, -1):
        @pl.when(beside(dc))
        def _(dc=dc):
            row_copy(dc).start()

    @pl.when(core == 0)
    def _():
        arrive(-1, False)
        arrive(-1, True)
        convolve(2, 0, 4, True, False)

    for dc in (1, -1):
        @pl.when(beside(-dc))
        def _(dc=dc):
            row_copy(dc).wait_recv()
            for ds in (1, -1):
                @pl.when(there(ds))
                def _(ds=ds):
                    pass_copy(ds, dc).start()
    activate(1)

    @pl.when(core == 1)
    def _():
        convolve(1, 0, 4, True, False)

    arrive(1, False)
    convolve(0, 0, 2, False, False)
    arrive(1, True)
    convolve(0, 2, 4, False, False)
    for n in range(2):
        @pl.when(core == 1)
        def _(n=n):
            arrive(-1, n == 1)
        convolve(1 + core, 2 * n, 2 * n + 2, False, True)

    @pl.when(above)
    def _():
        def go(pair, carry):
            low_copy(pair).wait_send()
            return carry

        lax.fori_loop(0, bands // 2, go, 0)
    for h in range(2):
        for u in range(2):
            for slot in range(2):
                stage(slot, h, u).wait_send()
            for v in range(2):
                relay_copy(h, u, v).wait_send()
    for ds in (1, -1):
        @pl.when(there(ds))
        def _(ds=ds):
            for h in range(2):
                for u in range(2):
                    for v in range(2):
                        halo_copy(ds, h, u, v).wait_send()
            for dc in (1, -1):
                @pl.when(beside(-dc))
                def _(dc=dc):
                    pass_copy(ds, dc).wait_send()
    for dc in (1, -1):
        @pl.when(beside(dc))
        def _(dc=dc):
            row_copy(dc).wait_send()


UNROLL = 2


def save(a_ref, b_ref, to_a, to_b, sems):
    one, two = pltpu.make_async_copy(a_ref, to_a, sems.at[0]), pltpu.make_async_copy(b_ref, to_b, sems.at[1])
    one.start()
    two.start()
    one.wait()
    two.wait()


def local_square(volume, weight_one, bias_one, weight_two, bias_two):
    c, planes, height, width = volume.shape
    k = weight_one.shape[4]
    parts, slabs = lax.axis_size("chan"), lax.axis_size("slab")
    deep = 256 // c
    bands = height // deep
    rows, cols = height // 2, width // 2
    mine = rows // parts
    vmem = pl.BlockSpec(memory_space=pltpu.VMEM)
    hbm = pl.BlockSpec(memory_space=pltpu.HBM)
    near = pl.BlockSpec(memory_space=pl.ANY)
    dma = pltpu.SemaphoreType.DMA
    block = jax.ShapeDtypeStruct((mine, cols, k), BF)
    act, grouped = pl.pallas_call(
        functools.partial(square, slabs),
        out_shape=(block, block),
        in_specs=[hbm] + [vmem] * 4,
        out_specs=(vmem, vmem),
        scratch_shapes=[
            pltpu.VMEM((planes, c, bands, deep, width), BF),
            pltpu.VMEM((c, bands, deep, width), BF),
            pltpu.VMEM((9, height * c // 128 + 1, cols, 128), BF),
            pltpu.VMEM((rows, cols, k), BF),
            pltpu.VMEM((parts - 1, mine, cols, k), BF),
            pltpu.VMEM((3, mine + 2, cols, k), BF),
            pltpu.VMEM((9 * 256, 64 // c * k), BF),
            pltpu.VMEM((3, 3, 3 * k, k), BF),
            pltpu.VMEM((3, mine * cols, k), F32),
            dma((2, 2)),
            dma((bands // 2,)), dma((bands // 2,)),
            dma((2, 2, 2)), dma((2, 2, 2)),
            dma((2, 2, 2)), dma((2, 2, 2)),
            dma((2, 2, 2, 2)), dma((2, 2, 2, 2)),
            dma((2,)), dma((2,)),
            dma((2, 2)), dma((2, 2)),
        ],
        compiler_params=pltpu.CompilerParams(vmem_limit_bytes=52 << 20, collective_id=0, has_side_effects=True),
    )(volume.reshape(c, planes, bands, deep, width), weight_one, bias_one.reshape(1, k), weight_two, bias_two.reshape(1, k))
    act, grouped = pl.pallas_call(
        save, out_shape=(block, block), in_specs=[near, near], out_specs=(hbm, hbm), scratch_shapes=[dma((2,))],
        compiler_params=pltpu.CompilerParams(vmem_limit_bytes=1 << 20),
    )(act, grouped)
    return act[None], grouped[None]


def body(parts, slabs, own_ref, k1_ref, b1_ref, k2_ref, b2_ref, act_ref, out_ref,
         low_ref, t_ref, part_ref, recv_ref, a_ref, w1_ref, w2_ref, acc_ref,
         low_send, low_recv, sum_send, sum_recv, halo_send, halo_recv):
    c = own_ref.shape[2]
    tall = 128 // c
    wins = own_ref.shape[1] // tall
    half = own_ref.shape[3] // 2
    mine, q, k = act_ref.shape
    outs = tall // 2
    step = 4 * outs if mine % (4 * outs) == 0 else mine
    pieces = mine // step
    me, slab = lax.axis_index("chan"), lax.axis_index("slab")

    def peer(s):
        if parts == 4:
            return 2 * lax.rem(me // 2 + lax.div(s, 2), 2) + lax.rem(lax.rem(me, 2) + lax.rem(s, 2), 2)
        return lax.rem(me + s, parts)

    def inside(dc, ds):
        ok = None
        for coord, move, size in ((me, dc, parts), (slab, ds, slabs)):
            if move:
                one = coord + move < size if move > 0 else coord + move >= 0
                ok = one if ok is None else jnp.logical_and(ok, one)
        return ok

    barrier = pltpu.get_barrier_semaphore()
    for s in range(1, parts):
        pl.semaphore_signal(barrier, inc=1, device_id={"chan": peer(jnp.int32(s)), "slab": slab}, device_id_type=MESH)
    for dc, ds in AROUND:
        if ds:
            @pl.when(inside(dc, ds))
            def _(dc=dc, ds=ds):
                pl.semaphore_signal(barrier, inc=1, device_id={"chan": me + dc, "slab": slab + ds}, device_id_type=MESH)
    one = jnp.int32(1)
    across = jnp.minimum(slab, one) + jnp.minimum(jnp.int32(slabs - 1) - slab, one)
    along = one + jnp.minimum(me, one) + jnp.minimum(jnp.int32(parts - 1) - me, one)
    pl.semaphore_wait(barrier, jnp.int32(parts - 1) + across * along)

    def low_copy():
        return pltpu.make_async_remote_copy(
            src_ref=own_ref.at[own_ref.shape[0] - 1], dst_ref=low_ref, send_sem=low_send, recv_sem=low_recv,
            device_id={"chan": me, "slab": slab + 1}, device_id_type=MESH)

    @pl.when(slab + 1 < slabs)
    def _():
        low_copy().start()

    w1_ref[...] = jnp.zeros_like(w1_ref)
    for e in range(9):
        i, l = divmod(e, 3)
        for par in range(outs):
            for j in range(3):
                start = e * 256 + (tall - 1 + 2 * par + j) * c
                w1_ref[start:start + c, par * k:(par + 1) * k] = k1_ref[i, j, l]
    m = k2_ref.shape[3]
    group = lax.broadcasted_iota(jnp.int32, (m, k), 1) // m
    for i in range(3):
        for l in range(3):
            for j in range(3):
                taps = k2_ref[i, j, l]
                for g in range(k // m):
                    w2_ref[i, l, j * k + g * m:j * k + (g + 1) * m] = jnp.where(group == g, taps, jnp.zeros_like(taps))
    width = own_ref.shape[3]
    spot = lax.broadcasted_iota(jnp.int32, (half, width), 1) - 2 * lax.broadcasted_iota(jnp.int32, (half, width), 0)
    sel = jnp.concatenate([jnp.where(spot == l - 1, 1.0, 0.0) for l in range(3)], axis=0).astype(BF)
    for e in range(9):
        t_ref[e, 0] = jnp.zeros_like(t_ref[e, 0])

    def decimate(d):
        def go(b, carry):
            rows = pl.ds(4 * tall * b, 4 * tall)
            x = low_ref[rows] if d == 0 else own_ref[d - 1, rows]
            x = x.reshape(512, own_ref.shape[3])
            t = lax.dot_general(sel, x, (((1,), (1,)), ((), ())), preferred_element_type=F32).astype(BF)
            for l in range(3):
                for u in range(4):
                    t_ref[3 * d + l, 4 * b + u + 1] = t[l * half:(l + 1) * half, 128 * u:128 * (u + 1)]
            return carry

        lax.fori_loop(0, wins // 4, go, 0)

    decimate(1)
    decimate(2)

    @pl.when(slab == 0)
    def _():
        low_ref[...] = jnp.zeros_like(low_ref)

    @pl.when(slab > 0)
    def _():
        low_copy().wait_recv()

    decimate(0)

    def chunk(b):
        lhs = []
        for e in range(9):
            lhs.append(t_ref[e, pl.ds(4 * b, 4)].reshape(4 * half, 128))
            lhs.append(t_ref[e, pl.ds(4 * b + 1, 4)].reshape(4 * half, 128))
        res = jnp.dot(jnp.concatenate(lhs, axis=1), w1_ref[...], preferred_element_type=F32).astype(BF)
        for u in range(4):
            for par in range(outs):
                part_ref[4 * outs * b + outs * u + par] = res[u * half:(u + 1) * half, par * k:(par + 1) * k]

    def sum_copy(s, h):
        to = peer(s)
        return pltpu.make_async_remote_copy(
            src_ref=part_ref.at[pl.ds(to * mine + h * step, step)], dst_ref=recv_ref.at[s - 1, pl.ds(h * step, step)],
            send_sem=sum_send.at[s - 1, h], recv_sem=sum_recv.at[s - 1, h],
            device_id={"chan": to, "slab": slab}, device_id_type=MESH)

    paired = parts == 4 and step == 4 * outs
    hop = step // 2

    def stage(slot, h, u):
        to = peer(jnp.int32(1 + u if slot < 2 else 2 - u))
        block = peer(jnp.int32(3)) if slot == 1 else to
        at = h * step + u * hop
        return pltpu.make_async_remote_copy(
            src_ref=part_ref.at[pl.ds(block * mine + at, hop)], dst_ref=recv_ref.at[slot, pl.ds(at, hop)],
            send_sem=sum_send.at[slot, 2 * h + u], recv_sem=sum_recv.at[slot, 2 * h + u],
            device_id={"chan": to, "slab": slab}, device_id_type=MESH)

    if paired:
        far, across_x, across_y = (peer(jnp.int32(s)) for s in (3, 1, 2))

        def first(h, carry):
            chunk(far * pieces + h)
            stage(1, h, 0).start()
            stage(1, h, 1).start()
            chunk(across_x * pieces + h)
            stage(0, h, 0).start()
            chunk(across_y * pieces + h)
            stage(0, h, 1).start()
            return carry

        lax.fori_loop(0, pieces, first, 0)
        for h in range(pieces):
            for u, block in ((0, across_y), (1, across_x)):
                at = h * step + u * hop
                stage(1, h, u).wait_recv()
                here = pl.ds(block * mine + at, hop)
                both = part_ref[here].astype(F32) + recv_ref[1, at:at + hop].astype(F32)
                part_ref[here] = both.astype(BF)
                stage(2, h, u).start()
            chunk(me * pieces + h)
    elif step == 4 * outs:
        def away(n, carry):
            s, h = parts - 1 - lax.rem(n, parts - 1), lax.div(n, parts - 1)
            chunk(peer(s) * pieces + h)
            sum_copy(s, h).start()
            return carry

        def home(h, carry):
            chunk(me * pieces + h)
            return carry

        lax.fori_loop(0, (parts - 1) * pieces, away, 0)
        lax.fori_loop(0, pieces, home, 0)
    else:
        def one(n, carry):
            chunk(n)
            return carry

        lax.fori_loop(0, wins // 4, one, 0)
        for s in range(1, parts):
            sum_copy(jnp.int32(s), 0).start()

    def spots(dc, ds, h):
        if dc == 0:
            rows = pl.ds(1 + h * step, step)
            return a_ref.at[1, rows], a_ref.at[1 - ds, rows]
        return a_ref.at[1, pl.ds(mine if dc > 0 else 1, 1)], a_ref.at[1 - ds, pl.ds(0 if dc > 0 else mine + 1, 1)]

    def halo_copy(n, h):
        dc, ds = AROUND[n]
        src, dst = spots(dc, ds, h)
        return pltpu.make_async_remote_copy(
            src_ref=src, dst_ref=dst, send_sem=halo_send.at[n, h], recv_sem=halo_recv.at[n, h],
            device_id={"chan": me + dc, "slab": slab + ds}, device_id_type=MESH)

    def due(dc):
        return range(pieces) if dc == 0 else (pieces - 1,) if dc > 0 else (0,)

    def arrive(n):
        dc, ds = AROUND[n]
        there = inside(-dc, -ds)
        for h in due(dc):
            @pl.when(there)
            def _(h=h):
                halo_copy(n, h).wait_recv()

            @pl.when(jnp.logical_not(there))
            def _(h=h):
                dst = spots(dc, ds, h)[1]
                dst[...] = jnp.zeros(dst.shape, BF)

    for h in range(pieces):
        for slot in (0, 2) if paired else ():
            stage(slot, h, 0).wait_recv()
            stage(slot, h, 1).wait_recv()
        for s in () if paired else range(1, parts):
            sum_copy(jnp.int32(s), h).wait_recv()
        for r in range(h * step, (h + 1) * step, 4):
            total = part_ref[pl.ds(me * mine + r, 4)].astype(F32)
            for slot in (0, 2) if paired else range(parts - 1):
                total += recv_ref[slot, r:r + 4].astype(F32)
            act = leaky(total + b1_ref[...]).astype(BF)
            act_ref[r:r + 4] = act
            a_ref[1, r + 1:r + 5] = act
        for n, (dc, ds) in enumerate(AROUND):
            if h in due(dc):
                @pl.when(inside(dc, ds))
                def _(n=n, h=h):
                    halo_copy(n, h).start()

    for i, last in ((1, False), (0, False), (2, True)):
        for n, (dc, ds) in enumerate(AROUND):
            if 1 - ds == i:
                arrive(n)

        def rows4(b, carry, i=i, last=last):
            lhs = jnp.concatenate([a_ref[i, pl.ds(4 * b + j, 4)].reshape(4 * q, k) for j in range(3)], axis=1)
            here = pl.ds(4 * q * b, 4 * q)
            accs = []
            for l in range(3):
                acc = jnp.dot(lhs, w2_ref[i, l], preferred_element_type=F32)
                if i != 1:
                    acc += acc_ref[l, here]
                accs.append(acc)
            if not last:
                for l in range(3):
                    acc_ref[l, here] = accs[l]
                return carry
            col = lax.rem(lax.broadcasted_iota(jnp.int32, (4 * q, k), 0), q)
            left = jnp.where(col == 0, 0.0, pltpu.roll(accs[0], 1, 0))
            right = jnp.where(col == q - 1, 0.0, pltpu.roll(accs[2], 4 * q - 1, 0))
            res = left + accs[1] + right + b2_ref[...]
            out_ref[pl.ds(4 * b, 4)] = res.reshape(4, q, k).astype(BF)
            return carry

        lax.fori_loop(0, mine // 4, rows4, 0)

    @pl.when(slab + 1 < slabs)
    def _():
        low_copy().wait_send()
    for s in range(1, parts):
        for h in range(pieces):
            if paired:
                stage(s - 1, h, 0).wait_send()
                stage(s - 1, h, 1).wait_send()
            else:
                sum_copy(jnp.int32(s), h).wait_send()
    for n, (dc, ds) in enumerate(AROUND):
        for h in due(dc):
            @pl.when(inside(dc, ds))
            def _(n=n, h=h):
                halo_copy(n, h).wait_send()


def local(volume, weight_one, bias_one, weight_two, bias_two):
    c, planes, height, width = volume.shape
    k = weight_one.shape[4]
    parts, slabs = lax.axis_size("chan"), lax.axis_size("slab")
    own_t = volume.transpose(1, 2, 0, 3)
    rows, cols = height // 2, width // 2
    mine = rows // parts
    step = 256 // c if mine % (256 // c) == 0 else mine
    vmem = pl.BlockSpec(memory_space=pltpu.VMEM)
    dma = pltpu.SemaphoreType.DMA
    block = jax.ShapeDtypeStruct((mine, cols, k), BF)
    act, grouped = pl.pallas_call(
        functools.partial(body, parts, slabs),
        out_shape=(block, block),
        in_specs=[vmem] * 5,
        out_specs=(vmem, vmem),
        scratch_shapes=[
            pltpu.VMEM((height, c, width), BF),
            pltpu.VMEM((9, height * c // 128 + 1, cols, 128), BF),
            pltpu.VMEM((rows, cols, k), BF),
            pltpu.VMEM((parts - 1, mine, cols, k), BF),
            pltpu.VMEM((3, mine + 2, cols, k), BF),
            pltpu.VMEM((9 * 256, 64 // c * k), BF),
            pltpu.VMEM((3, 3, 3 * k, k), BF),
            pltpu.VMEM((3, mine * cols, k), F32),
            dma, dma,
            dma((parts - 1, 2 * mine // step)), dma((parts - 1, 2 * mine // step)),
            dma((8, mine // step)), dma((8, mine // step)),
        ],
        compiler_params=pltpu.CompilerParams(vmem_limit_bytes=48 << 20, collective_id=0, has_side_effects=True),
    )(own_t, weight_one, bias_one.reshape(1, k), weight_two, bias_two.reshape(1, k))
    return act[None], grouped[None]


def solution(mesh):
    in_specs = (P("chan", "slab", None, None), P(None, None, None, "chan", None), P(), P(), P())
    out_specs = (P("slab", "chan", None, None), P("slab", "chan", None, None))
    run = local_square if mesh.shape["chan"] == 4 else local
    return jax.shard_map(run, mesh=mesh, in_specs=in_specs, out_specs=out_specs, check_vma=False)
```

```python
import functools

import jax
import jax.numpy as jnp
from jax import lax
from jax.experimental import pallas as pl
from jax.experimental.pallas import tpu as pltpu
from jax.sharding import PartitionSpec as P

BF = jnp.bfloat16
F32 = jnp.float32
MESH = pl.DeviceIdType.MESH
AROUND = [(0, 1), (0, -1), (1, 0), (-1, 0), (1, 1), (1, -1), (-1, 1), (-1, -1)]


def leaky(value):
    return jnp.where(value > 0, value, 0.3 * value)


def square(slabs, vol_ref, k1_hbm, b1_hbm, k2_hbm, b2_hbm, act_ref, out_ref,
           x_ref, k1_ref, k2_ref, b1_ref, b2_ref,
           low_ref, t_ref, part_ref, recv_ref, a_ref, even_ref, odd_ref, w2_ref, acc_ref,
           load_sem, small_sem, low_send, low_recv, sum_send, sum_recv,
           halo_send, halo_recv, row_send, row_recv, pass_send, pass_recv):
    parts = 4
    c, _, bands, deep, width = vol_ref.shape
    mine, q, k = act_ref.shape
    half = width // 2
    me, slab = lax.axis_index("chan"), lax.axis_index("slab")
    core = lax.rem(slab, 2)

    def peer(s):
        return 2 * lax.rem(me // 2 + lax.div(s, 2), 2) + lax.rem(lax.rem(me, 2) + lax.rem(s, 2), 2)

    def turn(n):
        return jnp.where(n == 0, 3, jnp.where(n == 3, 0, n))

    far, across_x, across_y = (peer(jnp.int32(s)) for s in (3, 1, 2))
    above, below = slab + 1 < slabs, slab > 0

    def there(ds):
        return above if ds > 0 else below

    barrier = pltpu.get_barrier_semaphore()
    for s in range(1, parts):
        pl.semaphore_signal(barrier, inc=1, device_id={"chan": peer(jnp.int32(s)), "slab": slab}, device_id_type=MESH)
    for ds in (1, -1):
        @pl.when(there(ds))
        def _(ds=ds):
            pl.semaphore_signal(barrier, inc=1, device_id={"chan": me, "slab": slab + ds}, device_id_type=MESH)

    def load(d):
        return pltpu.make_async_copy(vol_ref.at[:, d], x_ref.at[d], load_sem.at[d])

    small = [pltpu.make_async_copy(a, b, small_sem.at[n]) for n, (a, b) in enumerate(
        ((k1_hbm, k1_ref), (k2_hbm, k2_ref), (b1_hbm, b1_ref), (b2_hbm, b2_ref)))]
    load(0).start()
    small[0].start()
    load(1).start()
    for n in range(1, 4):
        small[n].start()

    size = c * deep
    to, of = (lax.broadcasted_iota(jnp.int32, (size, size), n) for n in range(2))
    perm = jnp.where(of == lax.rem(to, c) * deep + lax.div(to, c), 1.0, 0.0).astype(BF)
    spot = lax.broadcasted_iota(jnp.int32, (half, width), 1) - 2 * lax.broadcasted_iota(jnp.int32, (half, width), 0)
    sel = jnp.concatenate([jnp.where(spot == l - 1, 1.0, 0.0) for l in range(3)], axis=0).astype(BF)
    for e in range(9):
        t_ref[e, 0] = jnp.zeros_like(t_ref[e, 0])
    even_ref[...] = jnp.zeros_like(even_ref)
    odd_ref[...] = jnp.zeros_like(odd_ref)

    def decimate(d, groups):
        source = low_ref if d == 0 else x_ref.at[d - 1]
        mixed = []
        for some in groups:
            x = [source[:, b].reshape(size, width) for b in some]
            mixed.append(jnp.dot(perm, jnp.concatenate(x, axis=1), preferred_element_type=F32).astype(BF))
        for some, x in zip(groups, mixed):
            for v, b in enumerate(some):
                t = lax.dot_general(sel, x[:, v * width:(v + 1) * width], (((1,), (1,)), ((), ())),
                                    preferred_element_type=F32).astype(BF)
                for l in range(3):
                    for g in range(2):
                        t_ref[3 * d + l, 2 * b + g + 1] = t[l * half:(l + 1) * half, 128 * g:128 * (g + 1)]

    def plane(d):
        load(d - 1).wait()
        decimate(d, [[b, b + 1] for b in range(0, bands, 2)])

    plane(1)
    small[0].wait()
    for e in range(9):
        i, l = divmod(e, 3)
        for j in range(3):
            start = e * 256 + (3 + j) * c
            even_ref[start:start + c] = k1_ref[i, j, l]
            start = e * 128 + (1 + j) * c
            odd_ref[start:start + c] = k1_ref[i, j, l]

    @pl.when(jnp.logical_not(below))
    def _():
        low_ref[...] = jnp.zeros_like(low_ref)
        a_ref[0] = jnp.zeros_like(a_ref[0])

    @pl.when(jnp.logical_not(above))
    def _():
        a_ref[2] = jnp.zeros_like(a_ref[2])

    for edge, row in ((0, 0), (parts - 1, mine + 1)):
        @pl.when(me == edge)
        def _(row=row):
            for i in range(3):
                a_ref[i, row] = jnp.zeros_like(a_ref[i, row])

    one = jnp.int32(1)
    across = jnp.minimum(slab, one) + jnp.minimum(jnp.int32(slabs - 1) - slab, one)
    pl.semaphore_wait(barrier, jnp.int32(parts - 1) + across)

    def low_copy(b):
        return pltpu.make_async_remote_copy(
            src_ref=vol_ref.at[:, 1, b], dst_ref=low_ref.at[:, b],
            send_sem=low_send.at[b], recv_sem=low_recv.at[b],
            device_id={"chan": me, "slab": slab + 1}, device_id_type=MESH)

    def place(r):
        s = 2 * lax.rem(me // 2 + lax.div(r, 2), 2) + lax.rem(lax.rem(me, 2) + lax.rem(r, 2), 2)
        return turn(s)

    def needed(n, act):
        r = peer(turn(n))
        early = jnp.logical_and(r > 0, place(jnp.maximum(r - 1, 0)) > n)
        late = jnp.logical_or(r == parts - 1, place(jnp.minimum(r + 1, parts - 1)) > n)

        @pl.when(early)
        def _():
            act(4 * r - 1)
        for b in range(3):
            act(4 * r + b)

        @pl.when(late)
        def _():
            act(4 * r + 3)

    @pl.when(above)
    def _():
        def go(n, carry):
            needed(n, lambda b: low_copy(b).start())
            return carry

        lax.fori_loop(0, parts, go, 0)

    plane(2)

    def spread():
        small[1].wait()
        m = k2_ref.shape[3]
        group = lax.broadcasted_iota(jnp.int32, (m, k), 1) // m
        for i in range(3):
            for l in range(3):
                for j in range(3):
                    taps = k2_ref[i, j, l]
                    for g in range(k // m):
                        at = (3 * i + j) * k + g * m
                        w2_ref[l, at:at + m] = jnp.where(group == g, taps, jnp.zeros_like(taps))

    def first(h, u):
        return 4 * h if u == 0 else 12 - 4 * h

    def row2(h, u, v):
        return first(h, u) + (2 * v if u == 0 else 2 - 2 * v)

    def chunk(r, runs):
        before, here = ([jnp.concatenate(
            [t_ref[e, pl.ds(8 * r + w + lag, n)].reshape(n * half, 128) for w, n in runs], axis=0)
            for e in range(9)] for lag in range(2))
        odd = jnp.dot(jnp.concatenate(here, axis=1), odd_ref[...], preferred_element_type=F32).astype(BF)
        both = [x for pair in zip(before, here) for x in pair]
        even = jnp.dot(jnp.concatenate(both, axis=1), even_ref[...], preferred_element_type=F32).astype(BF)
        for at, w in enumerate([w + m for w, n in runs for m in range(n)]):
            part_ref[mine * r + 2 * w] = even[at * half:(at + 1) * half]
            part_ref[mine * r + 2 * w + 1] = odd[at * half:(at + 1) * half]

    def stage(slot, h, u, v):
        to = peer(jnp.int32(1 + u if slot < 2 else 2 - u))
        block = far if slot == 1 else to
        at = row2(h, u, v)
        return pltpu.make_async_remote_copy(
            src_ref=part_ref.at[pl.ds(block * mine + at, 2)], dst_ref=recv_ref.at[slot, pl.ds(at, 2)],
            send_sem=sum_send.at[slot, h, u, v], recv_sem=sum_recv.at[slot, h, u, v],
            device_id={"chan": to, "slab": slab}, device_id_type=MESH)

    def relay(h, v):
        for u, block in ((0, across_y), (1, across_x)):
            stage(1, h, u, v).wait_recv()
            at = row2(h, u, v)
            here = pl.ds(block * mine + at, 2)
            both = part_ref[here].astype(F32) + recv_ref[1, pl.ds(at, 2)].astype(F32)
            part_ref[here] = both.astype(BF)
            stage(2, h, u, v).start()

    def fetch(n):
        r = peer(turn(n))

        @pl.when(below)
        def _():
            needed(n, lambda b: low_copy(b).wait_recv())

        decimate(0, [[jnp.maximum(4 * r - 1, 0), 4 * r], [4 * r + 1, 4 * r + 2], [4 * r + 3]])
        return r

    def send(slot, h, v):
        for u in range(2):
            stage(slot, h, u, v).start()

    def near(n, carry):
        chunk(fetch(n), ((0, 8),))

        @pl.when(n == 1)
        def _():
            stage(0, 0, 0, 0).start()

        @pl.when(n == 2)
        def _():
            stage(0, 0, 1, 0).start()
        return carry

    def halo_copy(ds, h, u, v):
        at = pl.ds(row2(h, u, v) + 1, 2)
        n = (1 - ds) // 2
        return pltpu.make_async_remote_copy(
            src_ref=a_ref.at[1, at], dst_ref=a_ref.at[1 - ds, at],
            send_sem=halo_send.at[n, h, u, v], recv_sem=halo_recv.at[n, h, u, v],
            device_id={"chan": me, "slab": slab + ds}, device_id_type=MESH)

    def row_copy(dc):
        n = (1 - dc) // 2
        return pltpu.make_async_remote_copy(
            src_ref=a_ref.at[1, pl.ds(mine if dc > 0 else 1, 1)], dst_ref=a_ref.at[1, pl.ds(0 if dc > 0 else mine + 1, 1)],
            send_sem=row_send.at[n], recv_sem=row_recv.at[n],
            device_id={"chan": me + dc, "slab": slab}, device_id_type=MESH)

    def pass_copy(ds, dc):
        n, e = (1 - ds) // 2, (1 - dc) // 2
        row = pl.ds(0 if dc > 0 else mine + 1, 1)
        return pltpu.make_async_remote_copy(
            src_ref=a_ref.at[1, row], dst_ref=a_ref.at[1 - ds, row],
            send_sem=pass_send.at[n, e], recv_sem=pass_recv.at[n, e],
            device_id={"chan": me, "slab": slab + ds}, device_id_type=MESH)

    def beside(dc):
        return me + 1 < parts if dc > 0 else me > 0

    def activate(h, v):
        for u in range(2):
            stage(0, h, u, v).wait_recv()
            stage(2, h, u, v).wait_recv()
            at = row2(h, u, v)
            total = part_ref[pl.ds(me * mine + at, 2)].astype(F32)
            for slot in (0, 2):
                total += recv_ref[slot, pl.ds(at, 2)].astype(F32)
            act = leaky(total + b1_ref[...]).astype(BF)
            act_ref[pl.ds(at, 2)] = act
            a_ref[1, pl.ds(at + 1, 2)] = act
            for ds in (1, -1):
                @pl.when(there(ds))
                def _(ds=ds, u=u):
                    halo_copy(ds, h, u, v).start()

    def arrive(ds, late):
        @pl.when(there(-ds))
        def _():
            for h in range(2):
                for v in range(2):
                    if (h == 1 and v == 1) == late:
                        for u in range(2):
                            halo_copy(ds, h, u, v).wait_recv()
            if not late:
                for dc in (1, -1):
                    @pl.when(beside(-dc))
                    def _(dc=dc):
                        pass_copy(ds, dc).wait_recv()

    def convolve(i, late, fresh, last):
        tops = (4, 8) if late else (0, 12)
        lhs = jnp.concatenate(
            [jnp.concatenate([a_ref[i, top + j:top + j + 4].reshape(4 * q, k) for top in tops], axis=0) for j in range(3)],
            axis=1)
        accs = [jnp.dot(lhs, w2_ref[l, 3 * k * i:3 * k * (i + 1)], preferred_element_type=F32) for l in range(3)]
        col = lax.rem(lax.broadcasted_iota(jnp.int32, (8 * q, k), 0), q)
        left = jnp.where(col == 0, 0.0, pltpu.roll(accs[0], 1, 0))
        right = jnp.where(col == q - 1, 0.0, pltpu.roll(accs[2], 8 * q - 1, 0))
        res = left + accs[1] + right
        res += b2_ref[...] if fresh else acc_ref[int(late)]
        if last:
            for n, top in enumerate(tops):
                out_ref[top:top + 4] = res[4 * q * n:4 * q * (n + 1)].reshape(4, q, k).astype(BF)
        else:
            acc_ref[int(late)] = res

    other = fetch(jnp.int32(0))
    for h, runs in enumerate((((0, 2), (6, 2)), ((2, 4),))):
        chunk(other, runs)
        for v in range(2):
            send(1, h, v)
    lax.fori_loop(1, parts - 1, near, 0)
    steps = [(h, v) for h in range(2) for v in range(2)]
    for n, (h, v) in enumerate(steps):
        relay(h, v)
        if n + 1 < len(steps):
            send(0, *steps[n + 1])
    spread()
    near(jnp.int32(parts - 1), 0)
    small[2].wait()
    small[3].wait()
    activate(0, 0)
    for dc in (1, -1):
        @pl.when(beside(dc))
        def _(dc=dc):
            row_copy(dc).start()
    activate(0, 1)
    activate(1, 0)

    for dc in (1, -1):
        @pl.when(beside(-dc))
        def _(dc=dc):
            row_copy(dc).wait_recv()
            for ds in (1, -1):
                @pl.when(there(ds))
                def _(ds=ds):
                    pass_copy(ds, dc).start()
    activate(1, 1)

    @pl.when(core == 0)
    def _():
        for late in (False, True):
            arrive(-1, late)
            convolve(2, late, True, False)
        for late in (False, True):
            convolve(1, late, False, False)
        for late in (False, True):
            arrive(1, late)
            convolve(0, late, False, True)

    @pl.when(core == 1)
    def _():
        for late in (False, True):
            convolve(1, late, True, False)
        for late in (False, True):
            arrive(1, late)
            convolve(0, late, False, False)
        for late in (False, True):
            arrive(-1, late)
            convolve(2, late, False, True)

    @pl.when(above)
    def _():
        def go(b, carry):
            low_copy(b).wait_send()
            return carry

        lax.fori_loop(0, bands, go, 0)
    for h in range(2):
        for u in range(2):
            for v in range(2):
                for slot in range(3):
                    stage(slot, h, u, v).wait_send()
    for ds in (1, -1):
        @pl.when(there(ds))
        def _(ds=ds):
            for h in range(2):
                for u in range(2):
                    for v in range(2):
                        halo_copy(ds, h, u, v).wait_send()
            for dc in (1, -1):
                @pl.when(beside(-dc))
                def _(dc=dc):
                    pass_copy(ds, dc).wait_send()
    for dc in (1, -1):
        @pl.when(beside(dc))
        def _(dc=dc):
            row_copy(dc).wait_send()


def save(a_ref, b_ref, to_a, to_b, sems):
    one, two = pltpu.make_async_copy(a_ref, to_a, sems.at[0]), pltpu.make_async_copy(b_ref, to_b, sems.at[1])
    one.start()
    two.start()
    one.wait()
    two.wait()


def local_square(volume, weight_one, bias_one, weight_two, bias_two):
    c, planes, height, width = volume.shape
    k = weight_one.shape[4]
    parts, slabs = lax.axis_size("chan"), lax.axis_size("slab")
    deep = 256 // c
    bands = height // deep
    rows, cols = height // 2, width // 2
    mine = rows // parts
    hbm = pl.BlockSpec(memory_space=pltpu.HBM)
    near = pl.BlockSpec(memory_space=pl.ANY)
    vmem = pl.BlockSpec(memory_space=pltpu.VMEM)
    dma = pltpu.SemaphoreType.DMA
    block = jax.ShapeDtypeStruct((mine, cols, k), BF)
    act, grouped = pl.pallas_call(
        functools.partial(square, slabs),
        out_shape=(pltpu.VMEM((mine, cols, k), BF),) * 2,
        in_specs=[hbm] * 5,
        out_specs=(vmem, vmem),
        scratch_shapes=[
            pltpu.VMEM((planes, c, bands, deep, width), BF),
            pltpu.VMEM(weight_one.shape, BF), pltpu.VMEM(weight_two.shape, BF),
            pltpu.VMEM((1, k), F32), pltpu.VMEM((1, k), F32),
            pltpu.VMEM((c, bands, deep, width), BF),
            pltpu.VMEM((9, height * c // 128 + 1, cols, 128), BF),
            pltpu.VMEM((rows, cols, k), BF),
            pltpu.VMEM((parts - 1, mine, cols, k), BF),
            pltpu.VMEM((3, mine + 2, cols, k), BF),
            pltpu.VMEM((9 * 256, k), BF),
            pltpu.VMEM((9 * 128, k), BF),
            pltpu.VMEM((3, 9 * k, k), BF),
            pltpu.VMEM((2, mine // 2 * cols, k), F32),
            dma((2,)), dma((4,)),
            dma((bands,)), dma((bands,)),
            dma((3, 2, 2, 2)), dma((3, 2, 2, 2)),
            dma((2, 2, 2, 2)), dma((2, 2, 2, 2)),
            dma((2,)), dma((2,)),
            dma((2, 2)), dma((2, 2)),
        ],
        compiler_params=pltpu.CompilerParams(vmem_limit_bytes=58 << 20, collective_id=0, has_side_effects=True),
    )(volume.reshape(c, planes, bands, deep, width), weight_one, bias_one.reshape(1, k), weight_two, bias_two.reshape(1, k))
    act, grouped = pl.pallas_call(
        save, out_shape=(block, block), in_specs=[near, near], out_specs=(hbm, hbm), scratch_shapes=[dma((2,))],
        compiler_params=pltpu.CompilerParams(vmem_limit_bytes=1 << 20),
    )(act, grouped)
    return act[None], grouped[None]


def body(parts, slabs, own_ref, k1_ref, b1_ref, k2_ref, b2_ref, act_ref, out_ref,
         low_ref, t_ref, part_ref, recv_ref, a_ref, w1_ref, w2_ref, acc_ref,
         low_send, low_recv, sum_send, sum_recv, halo_send, halo_recv):
    c = own_ref.shape[2]
    tall = 128 // c
    wins = own_ref.shape[1] // tall
    half = own_ref.shape[3] // 2
    mine, q, k = act_ref.shape
    outs = tall // 2
    step = 4 * outs if mine % (4 * outs) == 0 else mine
    pieces = mine // step
    me, slab = lax.axis_index("chan"), lax.axis_index("slab")

    def peer(s):
        if parts == 4:
            return 2 * lax.rem(me // 2 + lax.div(s, 2), 2) + lax.rem(lax.rem(me, 2) + lax.rem(s, 2), 2)
        return lax.rem(me + s, parts)

    def inside(dc, ds):
        ok = None
        for coord, move, size in ((me, dc, parts), (slab, ds, slabs)):
            if move:
                one = coord + move < size if move > 0 else coord + move >= 0
                ok = one if ok is None else jnp.logical_and(ok, one)
        return ok

    barrier = pltpu.get_barrier_semaphore()
    for s in range(1, parts):
        pl.semaphore_signal(barrier, inc=1, device_id={"chan": peer(jnp.int32(s)), "slab": slab}, device_id_type=MESH)
    for dc, ds in AROUND:
        if ds:
            @pl.when(inside(dc, ds))
            def _(dc=dc, ds=ds):
                pl.semaphore_signal(barrier, inc=1, device_id={"chan": me + dc, "slab": slab + ds}, device_id_type=MESH)
    one = jnp.int32(1)
    across = jnp.minimum(slab, one) + jnp.minimum(jnp.int32(slabs - 1) - slab, one)
    along = one + jnp.minimum(me, one) + jnp.minimum(jnp.int32(parts - 1) - me, one)
    pl.semaphore_wait(barrier, jnp.int32(parts - 1) + across * along)

    def low_copy():
        return pltpu.make_async_remote_copy(
            src_ref=own_ref.at[own_ref.shape[0] - 1], dst_ref=low_ref, send_sem=low_send, recv_sem=low_recv,
            device_id={"chan": me, "slab": slab + 1}, device_id_type=MESH)

    @pl.when(slab + 1 < slabs)
    def _():
        low_copy().start()

    w1_ref[...] = jnp.zeros_like(w1_ref)
    for e in range(9):
        i, l = divmod(e, 3)
        for par in range(outs):
            for j in range(3):
                start = e * 256 + (tall - 1 + 2 * par + j) * c
                w1_ref[start:start + c, par * k:(par + 1) * k] = k1_ref[i, j, l]
    m = k2_ref.shape[3]
    group = lax.broadcasted_iota(jnp.int32, (m, k), 1) // m
    for i in range(3):
        for l in range(3):
            for j in range(3):
                taps = k2_ref[i, j, l]
                for g in range(k // m):
                    w2_ref[i, l, j * k + g * m:j * k + (g + 1) * m] = jnp.where(group == g, taps, jnp.zeros_like(taps))
    width = own_ref.shape[3]
    spot = lax.broadcasted_iota(jnp.int32, (half, width), 1) - 2 * lax.broadcasted_iota(jnp.int32, (half, width), 0)
    sel = jnp.concatenate([jnp.where(spot == l - 1, 1.0, 0.0) for l in range(3)], axis=0).astype(BF)
    for e in range(9):
        t_ref[e, 0] = jnp.zeros_like(t_ref[e, 0])

    def decimate(d):
        def go(b, carry):
            rows = pl.ds(4 * tall * b, 4 * tall)
            x = low_ref[rows] if d == 0 else own_ref[d - 1, rows]
            x = x.reshape(512, own_ref.shape[3])
            t = lax.dot_general(sel, x, (((1,), (1,)), ((), ())), preferred_element_type=F32).astype(BF)
            for l in range(3):
                for u in range(4):
                    t_ref[3 * d + l, 4 * b + u + 1] = t[l * half:(l + 1) * half, 128 * u:128 * (u + 1)]
            return carry

        lax.fori_loop(0, wins // 4, go, 0)

    decimate(1)
    decimate(2)

    @pl.when(slab == 0)
    def _():
        low_ref[...] = jnp.zeros_like(low_ref)

    @pl.when(slab > 0)
    def _():
        low_copy().wait_recv()

    decimate(0)

    def chunk(b):
        lhs = []
        for e in range(9):
            lhs.append(t_ref[e, pl.ds(4 * b, 4)].reshape(4 * half, 128))
            lhs.append(t_ref[e, pl.ds(4 * b + 1, 4)].reshape(4 * half, 128))
        res = jnp.dot(jnp.concatenate(lhs, axis=1), w1_ref[...], preferred_element_type=F32).astype(BF)
        for u in range(4):
            for par in range(outs):
                part_ref[4 * outs * b + outs * u + par] = res[u * half:(u + 1) * half, par * k:(par + 1) * k]

    def sum_copy(s, h):
        to = peer(s)
        return pltpu.make_async_remote_copy(
            src_ref=part_ref.at[pl.ds(to * mine + h * step, step)], dst_ref=recv_ref.at[s - 1, pl.ds(h * step, step)],
            send_sem=sum_send.at[s - 1, h], recv_sem=sum_recv.at[s - 1, h],
            device_id={"chan": to, "slab": slab}, device_id_type=MESH)

    paired = parts == 4 and step == 4 * outs
    hop = step // 2

    def stage(slot, h, u):
        to = peer(jnp.int32(1 + u if slot < 2 else 2 - u))
        block = peer(jnp.int32(3)) if slot == 1 else to
        at = h * step + u * hop
        return pltpu.make_async_remote_copy(
            src_ref=part_ref.at[pl.ds(block * mine + at, hop)], dst_ref=recv_ref.at[slot, pl.ds(at, hop)],
            send_sem=sum_send.at[slot, 2 * h + u], recv_sem=sum_recv.at[slot, 2 * h + u],
            device_id={"chan": to, "slab": slab}, device_id_type=MESH)

    if paired:
        far, across_x, across_y = (peer(jnp.int32(s)) for s in (3, 1, 2))

        def first(h, carry):
            chunk(far * pieces + h)
            stage(1, h, 0).start()
            stage(1, h, 1).start()
            chunk(across_x * pieces + h)
            stage(0, h, 0).start()
            chunk(across_y * pieces + h)
            stage(0, h, 1).start()
            return carry

        lax.fori_loop(0, pieces, first, 0)
        for h in range(pieces):
            for u, block in ((0, across_y), (1, across_x)):
                at = h * step + u * hop
                stage(1, h, u).wait_recv()
                here = pl.ds(block * mine + at, hop)
                both = part_ref[here].astype(F32) + recv_ref[1, at:at + hop].astype(F32)
                part_ref[here] = both.astype(BF)
                stage(2, h, u).start()
            chunk(me * pieces + h)
    elif step == 4 * outs:
        def away(n, carry):
            s, h = parts - 1 - lax.rem(n, parts - 1), lax.div(n, parts - 1)
            chunk(peer(s) * pieces + h)
            sum_copy(s, h).start()
            return carry

        def home(h, carry):
            chunk(me * pieces + h)
            return carry

        lax.fori_loop(0, (parts - 1) * pieces, away, 0)
        lax.fori_loop(0, pieces, home, 0)
    else:
        def one(n, carry):
            chunk(n)
            return carry

        lax.fori_loop(0, wins // 4, one, 0)
        for s in range(1, parts):
            sum_copy(jnp.int32(s), 0).start()

    def spots(dc, ds, h):
        if dc == 0:
            rows = pl.ds(1 + h * step, step)
            return a_ref.at[1, rows], a_ref.at[1 - ds, rows]
        return a_ref.at[1, pl.ds(mine if dc > 0 else 1, 1)], a_ref.at[1 - ds, pl.ds(0 if dc > 0 else mine + 1, 1)]

    def halo_copy(n, h):
        dc, ds = AROUND[n]
        src, dst = spots(dc, ds, h)
        return pltpu.make_async_remote_copy(
            src_ref=src, dst_ref=dst, send_sem=halo_send.at[n, h], recv_sem=halo_recv.at[n, h],
            device_id={"chan": me + dc, "slab": slab + ds}, device_id_type=MESH)

    def due(dc):
        return range(pieces) if dc == 0 else (pieces - 1,) if dc > 0 else (0,)

    def arrive(n):
        dc, ds = AROUND[n]
        there = inside(-dc, -ds)
        for h in due(dc):
            @pl.when(there)
            def _(h=h):
                halo_copy(n, h).wait_recv()

            @pl.when(jnp.logical_not(there))
            def _(h=h):
                dst = spots(dc, ds, h)[1]
                dst[...] = jnp.zeros(dst.shape, BF)

    for h in range(pieces):
        for slot in (0, 2) if paired else ():
            stage(slot, h, 0).wait_recv()
            stage(slot, h, 1).wait_recv()
        for s in () if paired else range(1, parts):
            sum_copy(jnp.int32(s), h).wait_recv()
        for r in range(h * step, (h + 1) * step, 4):
            total = part_ref[pl.ds(me * mine + r, 4)].astype(F32)
            for slot in (0, 2) if paired else range(parts - 1):
                total += recv_ref[slot, r:r + 4].astype(F32)
            act = leaky(total + b1_ref[...]).astype(BF)
            act_ref[r:r + 4] = act
            a_ref[1, r + 1:r + 5] = act
        for n, (dc, ds) in enumerate(AROUND):
            if h in due(dc):
                @pl.when(inside(dc, ds))
                def _(n=n, h=h):
                    halo_copy(n, h).start()

    for i, last in ((1, False), (0, False), (2, True)):
        for n, (dc, ds) in enumerate(AROUND):
            if 1 - ds == i:
                arrive(n)

        def rows4(b, carry, i=i, last=last):
            lhs = jnp.concatenate([a_ref[i, pl.ds(4 * b + j, 4)].reshape(4 * q, k) for j in range(3)], axis=1)
            here = pl.ds(4 * q * b, 4 * q)
            accs = []
            for l in range(3):
                acc = jnp.dot(lhs, w2_ref[i, l], preferred_element_type=F32)
                if i != 1:
                    acc += acc_ref[l, here]
                accs.append(acc)
            if not last:
                for l in range(3):
                    acc_ref[l, here] = accs[l]
                return carry
            col = lax.rem(lax.broadcasted_iota(jnp.int32, (4 * q, k), 0), q)
            left = jnp.where(col == 0, 0.0, pltpu.roll(accs[0], 1, 0))
            right = jnp.where(col == q - 1, 0.0, pltpu.roll(accs[2], 4 * q - 1, 0))
            res = left + accs[1] + right + b2_ref[...]
            out_ref[pl.ds(4 * b, 4)] = res.reshape(4, q, k).astype(BF)
            return carry

        lax.fori_loop(0, mine // 4, rows4, 0)

    @pl.when(slab + 1 < slabs)
    def _():
        low_copy().wait_send()
    for s in range(1, parts):
        for h in range(pieces):
            if paired:
                stage(s - 1, h, 0).wait_send()
                stage(s - 1, h, 1).wait_send()
            else:
                sum_copy(jnp.int32(s), h).wait_send()
    for n, (dc, ds) in enumerate(AROUND):
        for h in due(dc):
            @pl.when(inside(dc, ds))
            def _(n=n, h=h):
                halo_copy(n, h).wait_send()


def local(volume, weight_one, bias_one, weight_two, bias_two):
    c, planes, height, width = volume.shape
    k = weight_one.shape[4]
    parts, slabs = lax.axis_size("chan"), lax.axis_size("slab")
    own_t = volume.transpose(1, 2, 0, 3)
    rows, cols = height // 2, width // 2
    mine = rows // parts
    step = 256 // c if mine % (256 // c) == 0 else mine
    vmem = pl.BlockSpec(memory_space=pltpu.VMEM)
    dma = pltpu.SemaphoreType.DMA
    block = jax.ShapeDtypeStruct((mine, cols, k), BF)
    act, grouped = pl.pallas_call(
        functools.partial(body, parts, slabs),
        out_shape=(block, block),
        in_specs=[vmem] * 5,
        out_specs=(vmem, vmem),
        scratch_shapes=[
            pltpu.VMEM((height, c, width), BF),
            pltpu.VMEM((9, height * c // 128 + 1, cols, 128), BF),
            pltpu.VMEM((rows, cols, k), BF),
            pltpu.VMEM((parts - 1, mine, cols, k), BF),
            pltpu.VMEM((3, mine + 2, cols, k), BF),
            pltpu.VMEM((9 * 256, 64 // c * k), BF),
            pltpu.VMEM((3, 3, 3 * k, k), BF),
            pltpu.VMEM((3, mine * cols, k), F32),
            dma, dma,
            dma((parts - 1, 2 * mine // step)), dma((parts - 1, 2 * mine // step)),
            dma((8, mine // step)), dma((8, mine // step)),
        ],
        compiler_params=pltpu.CompilerParams(vmem_limit_bytes=48 << 20, collective_id=0, has_side_effects=True),
    )(own_t, weight_one, bias_one.reshape(1, k), weight_two, bias_two.reshape(1, k))
    return act[None], grouped[None]


def solution(mesh):
    in_specs = (P("chan", "slab", None, None), P(None, None, None, "chan", None), P(), P(), P())
    out_specs = (P("slab", "chan", None, None), P("slab", "chan", None, None))
    run = local_square if mesh.shape["chan"] == 4 else local
    return jax.shard_map(run, mesh=mesh, in_specs=in_specs, out_specs=out_specs, check_vma=False)
```

```python
import functools

import jax
import jax.numpy as jnp
from jax import lax
from jax.experimental import pallas as pl
from jax.experimental.pallas import tpu as pltpu
from jax.sharding import PartitionSpec as P

BF = jnp.bfloat16
F32 = jnp.float32
MESH = pl.DeviceIdType.MESH
AROUND = [(0, 1), (0, -1), (1, 0), (-1, 0), (1, 1), (1, -1), (-1, 1), (-1, -1)]


def leaky(value):
    return jnp.where(value > 0, value, 0.3 * value)


def square(slabs, vol_ref, k1_hbm, b1_hbm, k2_hbm, b2_hbm, act_ref, out_ref,
           x_ref, k1_ref, k2_ref, b1_ref, b2_ref,
           low_ref, t_ref, part_ref, recv_ref, a_ref, even_ref, odd_ref, w2_ref, acc_ref,
           load_sem, small_sem, low_send, low_recv, sum_send, sum_recv,
           halo_send, halo_recv, row_send, row_recv, pass_send, pass_recv):
    parts = 4
    c, _, bands, deep, width = vol_ref.shape
    mine, q, k = act_ref.shape
    half = width // 2
    me, slab = lax.axis_index("chan"), lax.axis_index("slab")
    core = lax.rem(slab, 2)

    def peer(s):
        return 2 * lax.rem(me // 2 + lax.div(s, 2), 2) + lax.rem(lax.rem(me, 2) + lax.rem(s, 2), 2)

    def turn(n):
        return jnp.where(n == 0, 3, jnp.where(n == 3, 0, n))

    far, across_x, across_y = (peer(jnp.int32(s)) for s in (3, 1, 2))
    above, below = slab + 1 < slabs, slab > 0

    def there(ds):
        return above if ds > 0 else below

    barrier = pltpu.get_barrier_semaphore()
    for s in range(1, parts):
        pl.semaphore_signal(barrier, inc=1, device_id={"chan": peer(jnp.int32(s)), "slab": slab}, device_id_type=MESH)
    for ds in (1, -1):
        @pl.when(there(ds))
        def _(ds=ds):
            pl.semaphore_signal(barrier, inc=1, device_id={"chan": me, "slab": slab + ds}, device_id_type=MESH)

    def load(d):
        return pltpu.make_async_copy(vol_ref.at[:, d], x_ref.at[d], load_sem.at[d])

    small = [pltpu.make_async_copy(a, b, small_sem.at[n]) for n, (a, b) in enumerate(
        ((k1_hbm, k1_ref), (k2_hbm, k2_ref), (b1_hbm, b1_ref), (b2_hbm, b2_ref)))]
    load(0).start()
    small[0].start()
    load(1).start()
    for n in range(1, 4):
        small[n].start()

    size = c * deep
    to, of = (lax.broadcasted_iota(jnp.int32, (size, size), n) for n in range(2))
    perm = jnp.where(of == lax.rem(to, c) * deep + lax.div(to, c), 1.0, 0.0).astype(BF)
    spot = lax.broadcasted_iota(jnp.int32, (half, width), 1) - 2 * lax.broadcasted_iota(jnp.int32, (half, width), 0)
    sel = jnp.concatenate([jnp.where(spot == l - 1, 1.0, 0.0) for l in range(3)], axis=0).astype(BF)
    for e in range(9):
        t_ref[e, 0] = jnp.zeros_like(t_ref[e, 0])
    even_ref[...] = jnp.zeros_like(even_ref)
    odd_ref[...] = jnp.zeros_like(odd_ref)

    def decimate(d, groups):
        source = low_ref if d == 0 else x_ref.at[d - 1]
        mixed = []
        for some in groups:
            x = [source[:, b].reshape(size, width) for b in some]
            mixed.append(jnp.dot(perm, jnp.concatenate(x, axis=1), preferred_element_type=F32).astype(BF))
        for some, x in zip(groups, mixed):
            for v, b in enumerate(some):
                t = lax.dot_general(sel, x[:, v * width:(v + 1) * width], (((1,), (1,)), ((), ())),
                                    preferred_element_type=F32).astype(BF)
                for l in range(3):
                    for g in range(2):
                        t_ref[3 * d + l, 2 * b + g + 1] = t[l * half:(l + 1) * half, 128 * g:128 * (g + 1)]

    def plane(d):
        load(d - 1).wait()
        decimate(d, [[b, b + 1] for b in range(0, bands, 2)])

    plane(1)
    small[0].wait()
    for e in range(9):
        i, l = divmod(e, 3)
        for j in range(3):
            start = e * 256 + (3 + j) * c
            even_ref[start:start + c] = k1_ref[i, j, l]
            start = e * 128 + (1 + j) * c
            odd_ref[start:start + c] = k1_ref[i, j, l]

    @pl.when(jnp.logical_not(below))
    def _():
        low_ref[...] = jnp.zeros_like(low_ref)
        a_ref[0] = jnp.zeros_like(a_ref[0])

    @pl.when(jnp.logical_not(above))
    def _():
        a_ref[2] = jnp.zeros_like(a_ref[2])

    for edge, row in ((0, 0), (parts - 1, mine + 1)):
        @pl.when(me == edge)
        def _(row=row):
            for i in range(3):
                a_ref[i, row] = jnp.zeros_like(a_ref[i, row])

    one = jnp.int32(1)
    across = jnp.minimum(slab, one) + jnp.minimum(jnp.int32(slabs - 1) - slab, one)
    pl.semaphore_wait(barrier, jnp.int32(parts - 1) + across)

    def low_copy(b):
        return pltpu.make_async_remote_copy(
            src_ref=vol_ref.at[:, 1, b], dst_ref=low_ref.at[:, b],
            send_sem=low_send.at[b], recv_sem=low_recv.at[b],
            device_id={"chan": me, "slab": slab + 1}, device_id_type=MESH)

    def place(r):
        s = 2 * lax.rem(me // 2 + lax.div(r, 2), 2) + lax.rem(lax.rem(me, 2) + lax.rem(r, 2), 2)
        return turn(s)

    def needed(n, act):
        r = peer(turn(n))
        early = jnp.logical_and(r > 0, place(jnp.maximum(r - 1, 0)) > n)
        late = jnp.logical_or(r == parts - 1, place(jnp.minimum(r + 1, parts - 1)) > n)

        @pl.when(early)
        def _():
            act(4 * r - 1)
        for b in range(3):
            act(4 * r + b)

        @pl.when(late)
        def _():
            act(4 * r + 3)

    @pl.when(above)
    def _():
        def go(n, carry):
            needed(n, lambda b: low_copy(b).start())
            return carry

        lax.fori_loop(0, parts, go, 0)

    plane(2)

    def spread():
        small[1].wait()
        m = k2_ref.shape[3]
        group = lax.broadcasted_iota(jnp.int32, (m, k), 1) // m
        for i in range(3):
            for l in range(3):
                for j in range(3):
                    taps = k2_ref[i, j, l]
                    for g in range(k // m):
                        at = (3 * i + j) * k + g * m
                        w2_ref[l, at:at + m] = jnp.where(group == g, taps, jnp.zeros_like(taps))

    def first(h, u):
        return 4 * h if u == 0 else 12 - 4 * h

    def row2(h, u, v):
        return first(h, u) + (2 * v if u == 0 else 2 - 2 * v)

    def chunk(r, runs):
        before, here = ([jnp.concatenate(
            [t_ref[e, pl.ds(8 * r + w + lag, n)].reshape(n * half, 128) for w, n in runs], axis=0)
            for e in range(9)] for lag in range(2))
        odd = jnp.dot(jnp.concatenate(here, axis=1), odd_ref[...], preferred_element_type=F32).astype(BF)
        both = [x for pair in zip(before, here) for x in pair]
        even = jnp.dot(jnp.concatenate(both, axis=1), even_ref[...], preferred_element_type=F32).astype(BF)
        for at, w in enumerate([w + m for w, n in runs for m in range(n)]):
            part_ref[mine * r + 2 * w] = even[at * half:(at + 1) * half]
            part_ref[mine * r + 2 * w + 1] = odd[at * half:(at + 1) * half]

    def stage(slot, h, u, v):
        to = peer(jnp.int32(1 + u if slot < 2 else 2 - u))
        block = far if slot == 1 else to
        at = row2(h, u, v)
        return pltpu.make_async_remote_copy(
            src_ref=part_ref.at[pl.ds(block * mine + at, 2)], dst_ref=recv_ref.at[slot, pl.ds(at, 2)],
            send_sem=sum_send.at[slot, h, u, v], recv_sem=sum_recv.at[slot, h, u, v],
            device_id={"chan": to, "slab": slab}, device_id_type=MESH)

    def relay(h, v):
        for u, block in ((0, across_y), (1, across_x)):
            stage(1, h, u, v).wait_recv()
            at = row2(h, u, v)
            here = pl.ds(block * mine + at, 2)
            both = part_ref[here].astype(F32) + recv_ref[1, pl.ds(at, 2)].astype(F32)
            part_ref[here] = both.astype(BF)
            stage(2, h, u, v).start()

    def fetch(n):
        r = peer(turn(n))

        @pl.when(below)
        def _():
            needed(n, lambda b: low_copy(b).wait_recv())

        decimate(0, [[jnp.maximum(4 * r - 1, 0), 4 * r], [4 * r + 1, 4 * r + 2], [4 * r + 3]])
        return r

    def send(slot, h, v):
        for u in range(2):
            stage(slot, h, u, v).start()

    def near(n, carry):
        chunk(fetch(n), ((0, 8),))

        @pl.when(n == 1)
        def _():
            stage(0, 0, 0, 0).start()

        @pl.when(n == 2)
        def _():
            stage(0, 0, 1, 0).start()
        return carry

    def halo_copy(ds, h, u, v):
        at = pl.ds(row2(h, u, v) + 1, 2)
        n = (1 - ds) // 2
        return pltpu.make_async_remote_copy(
            src_ref=a_ref.at[1, at], dst_ref=a_ref.at[1 - ds, at],
            send_sem=halo_send.at[n, h, u, v], recv_sem=halo_recv.at[n, h, u, v],
            device_id={"chan": me, "slab": slab + ds}, device_id_type=MESH)

    def row_copy(dc):
        n = (1 - dc) // 2
        return pltpu.make_async_remote_copy(
            src_ref=a_ref.at[1, pl.ds(mine if dc > 0 else 1, 1)], dst_ref=a_ref.at[1, pl.ds(0 if dc > 0 else mine + 1, 1)],
            send_sem=row_send.at[n], recv_sem=row_recv.at[n],
            device_id={"chan": me + dc, "slab": slab}, device_id_type=MESH)

    def pass_copy(ds, dc):
        n, e = (1 - ds) // 2, (1 - dc) // 2
        row = pl.ds(0 if dc > 0 else mine + 1, 1)
        return pltpu.make_async_remote_copy(
            src_ref=a_ref.at[1, row], dst_ref=a_ref.at[1 - ds, row],
            send_sem=pass_send.at[n, e], recv_sem=pass_recv.at[n, e],
            device_id={"chan": me, "slab": slab + ds}, device_id_type=MESH)

    def beside(dc):
        return me + 1 < parts if dc > 0 else me > 0

    def activate(h, v):
        for u in range(2):
            stage(0, h, u, v).wait_recv()
            stage(2, h, u, v).wait_recv()
            at = row2(h, u, v)
            total = part_ref[pl.ds(me * mine + at, 2)].astype(F32)
            for slot in (0, 2):
                total += recv_ref[slot, pl.ds(at, 2)].astype(F32)
            act = leaky(total + b1_ref[...]).astype(BF)
            act_ref[pl.ds(at, 2)] = act
            a_ref[1, pl.ds(at + 1, 2)] = act
            for ds in (1, -1):
                @pl.when(there(ds))
                def _(ds=ds, u=u):
                    halo_copy(ds, h, u, v).start()

    def arrive(ds, edges):
        @pl.when(there(-ds))
        def _():
            if edges:
                for dc in (1, -1):
                    @pl.when(beside(-dc))
                    def _(dc=dc):
                        pass_copy(ds, dc).wait_recv()
                return
            for h, v in steps:
                for u in range(2):
                    halo_copy(ds, h, u, v).wait_recv()

    steps = [(h, v) for h in range(2) for v in range(2)]

    def convolve(i, late, fresh, last):
        tops = (4, 8) if late else (0, 12)
        lhs = jnp.concatenate(
            [jnp.concatenate([a_ref[i, top + j:top + j + 4].reshape(4 * q, k) for top in tops], axis=0) for j in range(3)],
            axis=1)
        accs = [jnp.dot(lhs, w2_ref[l, 3 * k * i:3 * k * (i + 1)], preferred_element_type=F32) for l in range(3)]
        col = lax.rem(lax.broadcasted_iota(jnp.int32, (8 * q, k), 0), q)
        left = jnp.where(col == 0, 0.0, pltpu.roll(accs[0], 1, 0))
        right = jnp.where(col == q - 1, 0.0, pltpu.roll(accs[2], 8 * q - 1, 0))
        res = left + accs[1] + right
        res += b2_ref[...] if fresh else acc_ref[int(late)]
        if last:
            for n, top in enumerate(tops):
                out_ref[top:top + 4] = res[4 * q * n:4 * q * (n + 1)].reshape(4, q, k).astype(BF)
        else:
            acc_ref[int(late)] = res

    other = fetch(jnp.int32(0))
    for h, runs in enumerate((((0, 2), (6, 2)), ((2, 4),))):
        chunk(other, runs)
        for v in range(2):
            send(1, h, v)
    lax.fori_loop(1, parts - 1, near, 0)
    for n, (h, v) in enumerate(steps):
        if n + 1 < len(steps):
            relay(h, v)
            send(0, *steps[n + 1])
    spread()
    near(jnp.int32(parts - 1), 0)
    small[2].wait()
    small[3].wait()
    activate(0, 0)
    for dc in (1, -1):
        @pl.when(beside(dc))
        def _(dc=dc):
            row_copy(dc).start()
    relay(1, 1)
    activate(0, 1)
    activate(1, 0)
    activate(1, 1)
    for dc in (1, -1):
        @pl.when(beside(-dc))
        def _(dc=dc):
            row_copy(dc).wait_recv()
            for ds in (1, -1):
                @pl.when(there(ds))
                def _(ds=ds):
                    pass_copy(ds, dc).start()

    @pl.when(core == 0)
    def _():
        for edges in (False, True):
            convolve(1, not edges, True, False)
        for edges in (False, True):
            arrive(-1, edges)
            convolve(2, not edges, False, False)
        for edges in (False, True):
            arrive(1, edges)
            convolve(0, not edges, False, True)

    @pl.when(core == 1)
    def _():
        for edges in (False, True):
            convolve(1, not edges, True, False)
        for edges in (False, True):
            arrive(1, edges)
            convolve(0, not edges, False, False)
        for edges in (False, True):
            arrive(-1, edges)
            convolve(2, not edges, False, True)

    @pl.when(above)
    def _():
        def go(b, carry):
            low_copy(b).wait_send()
            return carry

        lax.fori_loop(0, bands, go, 0)
    for h in range(2):
        for u in range(2):
            for v in range(2):
                for slot in range(3):
                    stage(slot, h, u, v).wait_send()
    for ds in (1, -1):
        @pl.when(there(ds))
        def _(ds=ds):
            for h in range(2):
                for u in range(2):
                    for v in range(2):
                        halo_copy(ds, h, u, v).wait_send()
            for dc in (1, -1):
                @pl.when(beside(-dc))
                def _(dc=dc):
                    pass_copy(ds, dc).wait_send()
    for dc in (1, -1):
        @pl.when(beside(dc))
        def _(dc=dc):
            row_copy(dc).wait_send()


def save(a_ref, b_ref, to_a, to_b, sems):
    one, two = pltpu.make_async_copy(a_ref, to_a, sems.at[0]), pltpu.make_async_copy(b_ref, to_b, sems.at[1])
    one.start()
    two.start()
    one.wait()
    two.wait()


def local_square(volume, weight_one, bias_one, weight_two, bias_two):
    c, planes, height, width = volume.shape
    k = weight_one.shape[4]
    parts, slabs = lax.axis_size("chan"), lax.axis_size("slab")
    deep = 256 // c
    bands = height // deep
    rows, cols = height // 2, width // 2
    mine = rows // parts
    hbm = pl.BlockSpec(memory_space=pltpu.HBM)
    near = pl.BlockSpec(memory_space=pl.ANY)
    vmem = pl.BlockSpec(memory_space=pltpu.VMEM)
    dma = pltpu.SemaphoreType.DMA
    block = jax.ShapeDtypeStruct((mine, cols, k), BF)
    act, grouped = pl.pallas_call(
        functools.partial(square, slabs),
        out_shape=(pltpu.VMEM((mine, cols, k), BF),) * 2,
        in_specs=[hbm] * 5,
        out_specs=(vmem, vmem),
        scratch_shapes=[
            pltpu.VMEM((planes, c, bands, deep, width), BF),
            pltpu.VMEM(weight_one.shape, BF), pltpu.VMEM(weight_two.shape, BF),
            pltpu.VMEM((1, k), F32), pltpu.VMEM((1, k), F32),
            pltpu.VMEM((c, bands, deep, width), BF),
            pltpu.VMEM((9, height * c // 128 + 1, cols, 128), BF),
            pltpu.VMEM((rows, cols, k), BF),
            pltpu.VMEM((parts - 1, mine, cols, k), BF),
            pltpu.VMEM((3, mine + 2, cols, k), BF),
            pltpu.VMEM((9 * 256, k), BF),
            pltpu.VMEM((9 * 128, k), BF),
            pltpu.VMEM((3, 9 * k, k), BF),
            pltpu.VMEM((2, mine // 2 * cols, k), F32),
            dma((2,)), dma((4,)),
            dma((bands,)), dma((bands,)),
            dma((3, 2, 2, 2)), dma((3, 2, 2, 2)),
            dma((2, 2, 2, 2)), dma((2, 2, 2, 2)),
            dma((2,)), dma((2,)),
            dma((2, 2)), dma((2, 2)),
        ],
        compiler_params=pltpu.CompilerParams(vmem_limit_bytes=58 << 20, collective_id=0, has_side_effects=True),
    )(volume.reshape(c, planes, bands, deep, width), weight_one, bias_one.reshape(1, k), weight_two, bias_two.reshape(1, k))
    act, grouped = pl.pallas_call(
        save, out_shape=(block, block), in_specs=[near, near], out_specs=(hbm, hbm), scratch_shapes=[dma((2,))],
        compiler_params=pltpu.CompilerParams(vmem_limit_bytes=1 << 20),
    )(act, grouped)
    return act[None], grouped[None]


def body(parts, slabs, own_ref, k1_ref, b1_ref, k2_ref, b2_ref, act_ref, out_ref,
         low_ref, t_ref, part_ref, recv_ref, a_ref, w1_ref, w2_ref, acc_ref,
         low_send, low_recv, sum_send, sum_recv, halo_send, halo_recv):
    c = own_ref.shape[2]
    tall = 128 // c
    wins = own_ref.shape[1] // tall
    half = own_ref.shape[3] // 2
    mine, q, k = act_ref.shape
    outs = tall // 2
    step = 4 * outs if mine % (4 * outs) == 0 else mine
    pieces = mine // step
    me, slab = lax.axis_index("chan"), lax.axis_index("slab")

    def peer(s):
        if parts == 4:
            return 2 * lax.rem(me // 2 + lax.div(s, 2), 2) + lax.rem(lax.rem(me, 2) + lax.rem(s, 2), 2)
        return lax.rem(me + s, parts)

    def inside(dc, ds):
        ok = None
        for coord, move, size in ((me, dc, parts), (slab, ds, slabs)):
            if move:
                one = coord + move < size if move > 0 else coord + move >= 0
                ok = one if ok is None else jnp.logical_and(ok, one)
        return ok

    barrier = pltpu.get_barrier_semaphore()
    for s in range(1, parts):
        pl.semaphore_signal(barrier, inc=1, device_id={"chan": peer(jnp.int32(s)), "slab": slab}, device_id_type=MESH)
    for dc, ds in AROUND:
        if ds:
            @pl.when(inside(dc, ds))
            def _(dc=dc, ds=ds):
                pl.semaphore_signal(barrier, inc=1, device_id={"chan": me + dc, "slab": slab + ds}, device_id_type=MESH)
    one = jnp.int32(1)
    across = jnp.minimum(slab, one) + jnp.minimum(jnp.int32(slabs - 1) - slab, one)
    along = one + jnp.minimum(me, one) + jnp.minimum(jnp.int32(parts - 1) - me, one)
    pl.semaphore_wait(barrier, jnp.int32(parts - 1) + across * along)

    def low_copy():
        return pltpu.make_async_remote_copy(
            src_ref=own_ref.at[own_ref.shape[0] - 1], dst_ref=low_ref, send_sem=low_send, recv_sem=low_recv,
            device_id={"chan": me, "slab": slab + 1}, device_id_type=MESH)

    @pl.when(slab + 1 < slabs)
    def _():
        low_copy().start()

    w1_ref[...] = jnp.zeros_like(w1_ref)
    for e in range(9):
        i, l = divmod(e, 3)
        for par in range(outs):
            for j in range(3):
                start = e * 256 + (tall - 1 + 2 * par + j) * c
                w1_ref[start:start + c, par * k:(par + 1) * k] = k1_ref[i, j, l]
    m = k2_ref.shape[3]
    group = lax.broadcasted_iota(jnp.int32, (m, k), 1) // m
    for i in range(3):
        for l in range(3):
            for j in range(3):
                taps = k2_ref[i, j, l]
                for g in range(k // m):
                    w2_ref[i, l, j * k + g * m:j * k + (g + 1) * m] = jnp.where(group == g, taps, jnp.zeros_like(taps))
    width = own_ref.shape[3]
    spot = lax.broadcasted_iota(jnp.int32, (half, width), 1) - 2 * lax.broadcasted_iota(jnp.int32, (half, width), 0)
    sel = jnp.concatenate([jnp.where(spot == l - 1, 1.0, 0.0) for l in range(3)], axis=0).astype(BF)
    for e in range(9):
        t_ref[e, 0] = jnp.zeros_like(t_ref[e, 0])

    def decimate(d):
        def go(b, carry):
            rows = pl.ds(4 * tall * b, 4 * tall)
            x = low_ref[rows] if d == 0 else own_ref[d - 1, rows]
            x = x.reshape(512, own_ref.shape[3])
            t = lax.dot_general(sel, x, (((1,), (1,)), ((), ())), preferred_element_type=F32).astype(BF)
            for l in range(3):
                for u in range(4):
                    t_ref[3 * d + l, 4 * b + u + 1] = t[l * half:(l + 1) * half, 128 * u:128 * (u + 1)]
            return carry

        lax.fori_loop(0, wins // 4, go, 0)

    decimate(1)
    decimate(2)

    @pl.when(slab == 0)
    def _():
        low_ref[...] = jnp.zeros_like(low_ref)

    @pl.when(slab > 0)
    def _():
        low_copy().wait_recv()

    decimate(0)

    def chunk(b):
        lhs = []
        for e in range(9):
            lhs.append(t_ref[e, pl.ds(4 * b, 4)].reshape(4 * half, 128))
            lhs.append(t_ref[e, pl.ds(4 * b + 1, 4)].reshape(4 * half, 128))
        res = jnp.dot(jnp.concatenate(lhs, axis=1), w1_ref[...], preferred_element_type=F32).astype(BF)
        for u in range(4):
            for par in range(outs):
                part_ref[4 * outs * b + outs * u + par] = res[u * half:(u + 1) * half, par * k:(par + 1) * k]

    def sum_copy(s, h):
        to = peer(s)
        return pltpu.make_async_remote_copy(
            src_ref=part_ref.at[pl.ds(to * mine + h * step, step)], dst_ref=recv_ref.at[s - 1, pl.ds(h * step, step)],
            send_sem=sum_send.at[s - 1, h], recv_sem=sum_recv.at[s - 1, h],
            device_id={"chan": to, "slab": slab}, device_id_type=MESH)

    paired = parts == 4 and step == 4 * outs
    hop = step // 2

    def stage(slot, h, u):
        to = peer(jnp.int32(1 + u if slot < 2 else 2 - u))
        block = peer(jnp.int32(3)) if slot == 1 else to
        at = h * step + u * hop
        return pltpu.make_async_remote_copy(
            src_ref=part_ref.at[pl.ds(block * mine + at, hop)], dst_ref=recv_ref.at[slot, pl.ds(at, hop)],
            send_sem=sum_send.at[slot, 2 * h + u], recv_sem=sum_recv.at[slot, 2 * h + u],
            device_id={"chan": to, "slab": slab}, device_id_type=MESH)

    if paired:
        far, across_x, across_y = (peer(jnp.int32(s)) for s in (3, 1, 2))

        def first(h, carry):
            chunk(far * pieces + h)
            stage(1, h, 0).start()
            stage(1, h, 1).start()
            chunk(across_x * pieces + h)
            stage(0, h, 0).start()
            chunk(across_y * pieces + h)
            stage(0, h, 1).start()
            return carry

        lax.fori_loop(0, pieces, first, 0)
        for h in range(pieces):
            for u, block in ((0, across_y), (1, across_x)):
                at = h * step + u * hop
                stage(1, h, u).wait_recv()
                here = pl.ds(block * mine + at, hop)
                both = part_ref[here].astype(F32) + recv_ref[1, at:at + hop].astype(F32)
                part_ref[here] = both.astype(BF)
                stage(2, h, u).start()
            chunk(me * pieces + h)
    elif step == 4 * outs:
        def away(n, carry):
            s, h = parts - 1 - lax.rem(n, parts - 1), lax.div(n, parts - 1)
            chunk(peer(s) * pieces + h)
            sum_copy(s, h).start()
            return carry

        def home(h, carry):
            chunk(me * pieces + h)
            return carry

        lax.fori_loop(0, (parts - 1) * pieces, away, 0)
        lax.fori_loop(0, pieces, home, 0)
    else:
        def one(n, carry):
            chunk(n)
            return carry

        lax.fori_loop(0, wins // 4, one, 0)
        for s in range(1, parts):
            sum_copy(jnp.int32(s), 0).start()

    def spots(dc, ds, h):
        if dc == 0:
            rows = pl.ds(1 + h * step, step)
            return a_ref.at[1, rows], a_ref.at[1 - ds, rows]
        return a_ref.at[1, pl.ds(mine if dc > 0 else 1, 1)], a_ref.at[1 - ds, pl.ds(0 if dc > 0 else mine + 1, 1)]

    def halo_copy(n, h):
        dc, ds = AROUND[n]
        src, dst = spots(dc, ds, h)
        return pltpu.make_async_remote_copy(
            src_ref=src, dst_ref=dst, send_sem=halo_send.at[n, h], recv_sem=halo_recv.at[n, h],
            device_id={"chan": me + dc, "slab": slab + ds}, device_id_type=MESH)

    def due(dc):
        return range(pieces) if dc == 0 else (pieces - 1,) if dc > 0 else (0,)

    def arrive(n):
        dc, ds = AROUND[n]
        there = inside(-dc, -ds)
        for h in due(dc):
            @pl.when(there)
            def _(h=h):
                halo_copy(n, h).wait_recv()

            @pl.when(jnp.logical_not(there))
            def _(h=h):
                dst = spots(dc, ds, h)[1]
                dst[...] = jnp.zeros(dst.shape, BF)

    for h in range(pieces):
        for slot in (0, 2) if paired else ():
            stage(slot, h, 0).wait_recv()
            stage(slot, h, 1).wait_recv()
        for s in () if paired else range(1, parts):
            sum_copy(jnp.int32(s), h).wait_recv()
        for r in range(h * step, (h + 1) * step, 4):
            total = part_ref[pl.ds(me * mine + r, 4)].astype(F32)
            for slot in (0, 2) if paired else range(parts - 1):
                total += recv_ref[slot, r:r + 4].astype(F32)
            act = leaky(total + b1_ref[...]).astype(BF)
            act_ref[r:r + 4] = act
            a_ref[1, r + 1:r + 5] = act
        for n, (dc, ds) in enumerate(AROUND):
            if h in due(dc):
                @pl.when(inside(dc, ds))
                def _(n=n, h=h):
                    halo_copy(n, h).start()

    for i, last in ((1, False), (0, False), (2, True)):
        for n, (dc, ds) in enumerate(AROUND):
            if 1 - ds == i:
                arrive(n)

        def rows4(b, carry, i=i, last=last):
            lhs = jnp.concatenate([a_ref[i, pl.ds(4 * b + j, 4)].reshape(4 * q, k) for j in range(3)], axis=1)
            here = pl.ds(4 * q * b, 4 * q)
            accs = []
            for l in range(3):
                acc = jnp.dot(lhs, w2_ref[i, l], preferred_element_type=F32)
                if i != 1:
                    acc += acc_ref[l, here]
                accs.append(acc)
            if not last:
                for l in range(3):
                    acc_ref[l, here] = accs[l]
                return carry
            col = lax.rem(lax.broadcasted_iota(jnp.int32, (4 * q, k), 0), q)
            left = jnp.where(col == 0, 0.0, pltpu.roll(accs[0], 1, 0))
            right = jnp.where(col == q - 1, 0.0, pltpu.roll(accs[2], 4 * q - 1, 0))
            res = left + accs[1] + right + b2_ref[...]
            out_ref[pl.ds(4 * b, 4)] = res.reshape(4, q, k).astype(BF)
            return carry

        lax.fori_loop(0, mine // 4, rows4, 0)

    @pl.when(slab + 1 < slabs)
    def _():
        low_copy().wait_send()
    for s in range(1, parts):
        for h in range(pieces):
            if paired:
                stage(s - 1, h, 0).wait_send()
                stage(s - 1, h, 1).wait_send()
            else:
                sum_copy(jnp.int32(s), h).wait_send()
    for n, (dc, ds) in enumerate(AROUND):
        for h in due(dc):
            @pl.when(inside(dc, ds))
            def _(n=n, h=h):
                halo_copy(n, h).wait_send()


def local(volume, weight_one, bias_one, weight_two, bias_two):
    c, planes, height, width = volume.shape
    k = weight_one.shape[4]
    parts, slabs = lax.axis_size("chan"), lax.axis_size("slab")
    own_t = volume.transpose(1, 2, 0, 3)
    rows, cols = height // 2, width // 2
    mine = rows // parts
    step = 256 // c if mine % (256 // c) == 0 else mine
    vmem = pl.BlockSpec(memory_space=pltpu.VMEM)
    dma = pltpu.SemaphoreType.DMA
    block = jax.ShapeDtypeStruct((mine, cols, k), BF)
    act, grouped = pl.pallas_call(
        functools.partial(body, parts, slabs),
        out_shape=(block, block),
        in_specs=[vmem] * 5,
        out_specs=(vmem, vmem),
        scratch_shapes=[
            pltpu.VMEM((height, c, width), BF),
            pltpu.VMEM((9, height * c // 128 + 1, cols, 128), BF),
            pltpu.VMEM((rows, cols, k), BF),
            pltpu.VMEM((parts - 1, mine, cols, k), BF),
            pltpu.VMEM((3, mine + 2, cols, k), BF),
            pltpu.VMEM((9 * 256, 64 // c * k), BF),
            pltpu.VMEM((3, 3, 3 * k, k), BF),
            pltpu.VMEM((3, mine * cols, k), F32),
            dma, dma,
            dma((parts - 1, 2 * mine // step)), dma((parts - 1, 2 * mine // step)),
            dma((8, mine // step)), dma((8, mine // step)),
        ],
        compiler_params=pltpu.CompilerParams(vmem_limit_bytes=48 << 20, collective_id=0, has_side_effects=True),
    )(own_t, weight_one, bias_one.reshape(1, k), weight_two, bias_two.reshape(1, k))
    return act[None], grouped[None]


def solution(mesh):
    in_specs = (P("chan", "slab", None, None), P(None, None, None, "chan", None), P(), P(), P())
    out_specs = (P("slab", "chan", None, None), P("slab", "chan", None, None))
    run = local_square if mesh.shape["chan"] == 4 else local
    return jax.shard_map(run, mesh=mesh, in_specs=in_specs, out_specs=out_specs, check_vma=False)
```

```python
import functools

import jax
import jax.numpy as jnp
from jax import lax
from jax.experimental import pallas as pl
from jax.experimental.pallas import tpu as pltpu
from jax.sharding import PartitionSpec as P

BF = jnp.bfloat16
F32 = jnp.float32
MESH = pl.DeviceIdType.MESH
AROUND = [(0, 1), (0, -1), (1, 0), (-1, 0), (1, 1), (1, -1), (-1, 1), (-1, -1)]


def leaky(value):
    return jnp.where(value > 0, value, 0.3 * value)


def square(slabs, vol_ref, k1_hbm, b1_hbm, k2_hbm, b2_hbm, act_ref, out_ref,
           x_ref, k1_ref, k2_ref, b1_ref, b2_ref,
           low_ref, t_ref, part_ref, recv_ref, a_ref, even_ref, odd_ref, w2_ref, acc_ref,
           load_sem, small_sem, low_send, low_recv, sum_send, sum_recv,
           halo_send, halo_recv, row_send, row_recv, pass_send, pass_recv):
    parts = 4
    c, _, bands, deep, width = vol_ref.shape
    mine, q, k = act_ref.shape
    half = width // 2
    me, slab = lax.axis_index("chan"), lax.axis_index("slab")
    core = lax.rem(slab, 2)

    def peer(s):
        return 2 * lax.rem(me // 2 + lax.div(s, 2), 2) + lax.rem(lax.rem(me, 2) + lax.rem(s, 2), 2)

    def turn(n):
        return jnp.where(n == 0, 3, jnp.where(n == 3, 0, n))

    far, across_x, across_y = (peer(jnp.int32(s)) for s in (3, 1, 2))
    above, below = slab + 1 < slabs, slab > 0

    def there(ds):
        return above if ds > 0 else below

    barrier = pltpu.get_barrier_semaphore()
    for s in range(1, parts):
        pl.semaphore_signal(barrier, inc=1, device_id={"chan": peer(jnp.int32(s)), "slab": slab}, device_id_type=MESH)
    for ds in (1, -1):
        @pl.when(there(ds))
        def _(ds=ds):
            pl.semaphore_signal(barrier, inc=1, device_id={"chan": me, "slab": slab + ds}, device_id_type=MESH)

    def load(d):
        return pltpu.make_async_copy(vol_ref.at[:, d], x_ref.at[d], load_sem.at[d])

    small = [pltpu.make_async_copy(a, b, small_sem.at[n]) for n, (a, b) in enumerate(
        ((k1_hbm, k1_ref), (k2_hbm, k2_ref), (b1_hbm, b1_ref), (b2_hbm, b2_ref)))]
    load(0).start()
    small[0].start()
    load(1).start()
    for n in range(1, 4):
        small[n].start()

    size = c * deep
    to, of = (lax.broadcasted_iota(jnp.int32, (size, size), n) for n in range(2))
    perm = jnp.where(of == lax.rem(to, c) * deep + lax.div(to, c), 1.0, 0.0).astype(BF)
    spot = lax.broadcasted_iota(jnp.int32, (half, width), 1) - 2 * lax.broadcasted_iota(jnp.int32, (half, width), 0)
    sel = jnp.concatenate([jnp.where(spot == l - 1, 1.0, 0.0) for l in range(3)], axis=0).astype(BF)
    for e in range(9):
        t_ref[e, 0] = jnp.zeros_like(t_ref[e, 0])
    even_ref[...] = jnp.zeros_like(even_ref)
    odd_ref[...] = jnp.zeros_like(odd_ref)

    def decimate(d, groups):
        source = low_ref if d == 0 else x_ref.at[d - 1]
        mixed = []
        for some in groups:
            x = [source[:, b].reshape(size, width) for b in some]
            mixed.append(jnp.dot(perm, jnp.concatenate(x, axis=1), preferred_element_type=F32).astype(BF))
        for some, x in zip(groups, mixed):
            for v, b in enumerate(some):
                t = lax.dot_general(sel, x[:, v * width:(v + 1) * width], (((1,), (1,)), ((), ())),
                                    preferred_element_type=F32).astype(BF)
                for l in range(3):
                    for g in range(2):
                        t_ref[3 * d + l, 2 * b + g + 1] = t[l * half:(l + 1) * half, 128 * g:128 * (g + 1)]

    def plane(d):
        load(d - 1).wait()
        decimate(d, [[b, b + 1] for b in range(0, bands, 2)])

    plane(1)
    small[0].wait()
    for e in range(9):
        i, l = divmod(e, 3)
        for j in range(3):
            start = e * 256 + (3 + j) * c
            even_ref[start:start + c] = k1_ref[i, j, l]
            start = e * 128 + (1 + j) * c
            odd_ref[start:start + c] = k1_ref[i, j, l]

    @pl.when(jnp.logical_not(below))
    def _():
        low_ref[...] = jnp.zeros_like(low_ref)
        a_ref[0] = jnp.zeros_like(a_ref[0])

    @pl.when(jnp.logical_not(above))
    def _():
        a_ref[2] = jnp.zeros_like(a_ref[2])

    for edge, row in ((0, 0), (parts - 1, mine + 1)):
        @pl.when(me == edge)
        def _(row=row):
            for i in range(3):
                a_ref[i, row] = jnp.zeros_like(a_ref[i, row])

    one = jnp.int32(1)
    across = jnp.minimum(slab, one) + jnp.minimum(jnp.int32(slabs - 1) - slab, one)
    pl.semaphore_wait(barrier, jnp.int32(parts - 1) + across)

    def low_copy(b):
        return pltpu.make_async_remote_copy(
            src_ref=vol_ref.at[:, 1, b], dst_ref=low_ref.at[:, b],
            send_sem=low_send.at[b], recv_sem=low_recv.at[b],
            device_id={"chan": me, "slab": slab + 1}, device_id_type=MESH)

    def place(r):
        s = 2 * lax.rem(me // 2 + lax.div(r, 2), 2) + lax.rem(lax.rem(me, 2) + lax.rem(r, 2), 2)
        return turn(s)

    def needed(n, act):
        r = peer(turn(n))
        early = jnp.logical_and(r > 0, place(jnp.maximum(r - 1, 0)) > n)
        late = jnp.logical_or(r == parts - 1, place(jnp.minimum(r + 1, parts - 1)) > n)

        @pl.when(early)
        def _():
            act(4 * r - 1)
        for b in range(3):
            act(4 * r + b)

        @pl.when(late)
        def _():
            act(4 * r + 3)

    @pl.when(above)
    def _():
        def go(n, carry):
            needed(n, lambda b: low_copy(b).start())
            return carry

        lax.fori_loop(0, parts, go, 0)

    plane(2)

    def spread():
        small[1].wait()
        m = k2_ref.shape[3]
        group = lax.broadcasted_iota(jnp.int32, (m, k), 1) // m
        for i in range(3):
            for l in range(3):
                for j in range(3):
                    taps = k2_ref[i, j, l]
                    for g in range(k // m):
                        at = (3 * i + j) * k + g * m
                        w2_ref[l, at:at + m] = jnp.where(group == g, taps, jnp.zeros_like(taps))

    def first(h, u):
        return 4 * h if u == 0 else 12 - 4 * h

    def row2(h, u, v):
        return first(h, u) + (2 * v if u == 0 else 2 - 2 * v)

    def chunk(r, runs):
        before, here = ([jnp.concatenate(
            [t_ref[e, pl.ds(8 * r + w + lag, n)].reshape(n * half, 128) for w, n in runs], axis=0)
            for e in range(9)] for lag in range(2))
        odd = jnp.dot(jnp.concatenate(here, axis=1), odd_ref[...], preferred_element_type=F32).astype(BF)
        both = [x for pair in zip(before, here) for x in pair]
        even = jnp.dot(jnp.concatenate(both, axis=1), even_ref[...], preferred_element_type=F32).astype(BF)
        for at, w in enumerate([w + m for w, n in runs for m in range(n)]):
            part_ref[mine * r + 2 * w] = even[at * half:(at + 1) * half]
            part_ref[mine * r + 2 * w + 1] = odd[at * half:(at + 1) * half]

    def stage(slot, h, u, v):
        to = peer(jnp.int32(1 + u if slot < 2 else 2 - u))
        block = far if slot == 1 else to
        at = row2(h, u, v)
        return pltpu.make_async_remote_copy(
            src_ref=part_ref.at[pl.ds(block * mine + at, 2)], dst_ref=recv_ref.at[slot, pl.ds(at, 2)],
            send_sem=sum_send.at[slot, h, u, v], recv_sem=sum_recv.at[slot, h, u, v],
            device_id={"chan": to, "slab": slab}, device_id_type=MESH)

    def relay(h, v):
        for u, block in ((0, across_y), (1, across_x)):
            stage(1, h, u, v).wait_recv()
            at = row2(h, u, v)
            here = pl.ds(block * mine + at, 2)
            both = part_ref[here].astype(F32) + recv_ref[1, pl.ds(at, 2)].astype(F32)
            part_ref[here] = both.astype(BF)
            stage(2, h, u, v).start()

    def fetch(n):
        r = peer(turn(n))

        @pl.when(below)
        def _():
            needed(n, lambda b: low_copy(b).wait_recv())

        decimate(0, [[jnp.maximum(4 * r - 1, 0), 4 * r], [4 * r + 1, 4 * r + 2], [4 * r + 3]])
        return r

    def send(slot, h, v):
        for u in range(2):
            stage(slot, h, u, v).start()

    def near(n, carry):
        chunk(fetch(n), ((0, 8),))

        @pl.when(n == 1)
        def _():
            stage(0, 0, 0, 0).start()

        @pl.when(n == 2)
        def _():
            stage(0, 0, 1, 0).start()
        return carry

    def halo_copy(ds, h, u, v):
        at = pl.ds(row2(h, u, v) + 1, 2)
        n = (1 - ds) // 2
        return pltpu.make_async_remote_copy(
            src_ref=a_ref.at[1, at], dst_ref=a_ref.at[1 - ds, at],
            send_sem=halo_send.at[n, h, u, v], recv_sem=halo_recv.at[n, h, u, v],
            device_id={"chan": me, "slab": slab + ds}, device_id_type=MESH)

    def row_copy(dc):
        n = (1 - dc) // 2
        return pltpu.make_async_remote_copy(
            src_ref=a_ref.at[1, pl.ds(mine if dc > 0 else 1, 1)], dst_ref=a_ref.at[1, pl.ds(0 if dc > 0 else mine + 1, 1)],
            send_sem=row_send.at[n], recv_sem=row_recv.at[n],
            device_id={"chan": me + dc, "slab": slab}, device_id_type=MESH)

    def pass_copy(ds, dc):
        n, e = (1 - ds) // 2, (1 - dc) // 2
        row = pl.ds(0 if dc > 0 else mine + 1, 1)
        return pltpu.make_async_remote_copy(
            src_ref=a_ref.at[1, row], dst_ref=a_ref.at[1 - ds, row],
            send_sem=pass_send.at[n, e], recv_sem=pass_recv.at[n, e],
            device_id={"chan": me, "slab": slab + ds}, device_id_type=MESH)

    def beside(dc):
        return me + 1 < parts if dc > 0 else me > 0

    def activate(h, v):
        for u in range(2):
            stage(0, h, u, v).wait_recv()
            stage(2, h, u, v).wait_recv()
            at = row2(h, u, v)
            total = part_ref[pl.ds(me * mine + at, 2)].astype(F32)
            for slot in (0, 2):
                total += recv_ref[slot, pl.ds(at, 2)].astype(F32)
            act = leaky(total + b1_ref[...]).astype(BF)
            act_ref[pl.ds(at, 2)] = act
            a_ref[1, pl.ds(at + 1, 2)] = act
            for ds in (1, -1):
                @pl.when(there(ds))
                def _(ds=ds, u=u):
                    halo_copy(ds, h, u, v).start()

    def arrive(ds, edges):
        @pl.when(there(-ds))
        def _():
            if edges:
                for dc in (1, -1):
                    @pl.when(beside(-dc))
                    def _(dc=dc):
                        pass_copy(ds, dc).wait_recv()
                return
            for h, v in steps:
                for u in range(2):
                    halo_copy(ds, h, u, v).wait_recv()

    steps = [(h, v) for h in range(2) for v in range(2)]

    def convolve(i, late, fresh, last):
        tops = (4, 8) if late else (0, 12)
        lhs = jnp.concatenate(
            [jnp.concatenate([a_ref[i, top + j:top + j + 4].reshape(4 * q, k) for top in tops], axis=0) for j in range(3)],
            axis=1)
        accs = [jnp.dot(lhs, w2_ref[l, 3 * k * i:3 * k * (i + 1)], preferred_element_type=F32) for l in range(3)]
        col = lax.broadcasted_iota(jnp.int32, (q, k), 0)
        res = []
        for n in range(8):
            left, centre, right = (acc[n * q:(n + 1) * q] for acc in accs)
            left = jnp.where(col == 0, 0.0, pltpu.roll(left, 1, 0))
            right = jnp.where(col == q - 1, 0.0, pltpu.roll(right, q - 1, 0))
            res.append(left + centre + right)
        res = jnp.concatenate(res, axis=0)
        res += b2_ref[...] if fresh else acc_ref[int(late)]
        if last:
            for n, top in enumerate(tops):
                out_ref[top:top + 4] = res[4 * q * n:4 * q * (n + 1)].reshape(4, q, k).astype(BF)
        else:
            acc_ref[int(late)] = res

    other = fetch(jnp.int32(0))
    for h, runs in enumerate((((0, 2), (6, 2)), ((2, 4),))):
        chunk(other, runs)
        for v in range(2):
            send(1, h, v)
    lax.fori_loop(1, parts - 1, near, 0)
    for n, (h, v) in enumerate(steps):
        if n + 1 < len(steps):
            relay(h, v)
            send(0, *steps[n + 1])
    spread()
    near(jnp.int32(parts - 1), 0)
    small[2].wait()
    small[3].wait()
    activate(0, 0)
    for dc in (1, -1):
        @pl.when(beside(dc))
        def _(dc=dc):
            row_copy(dc).start()
    relay(1, 1)
    activate(0, 1)
    activate(1, 0)
    activate(1, 1)
    for dc in (1, -1):
        @pl.when(beside(-dc))
        def _(dc=dc):
            row_copy(dc).wait_recv()
            for ds in (1, -1):
                @pl.when(there(ds))
                def _(ds=ds):
                    pass_copy(ds, dc).start()

    @pl.when(core == 0)
    def _():
        for edges in (False, True):
            convolve(1, not edges, True, False)
        for edges in (False, True):
            arrive(-1, edges)
            convolve(2, not edges, False, False)
        for edges in (False, True):
            arrive(1, edges)
            convolve(0, not edges, False, True)

    @pl.when(core == 1)
    def _():
        for edges in (False, True):
            convolve(1, not edges, True, False)
        for edges in (False, True):
            arrive(1, edges)
            convolve(0, not edges, False, False)
        for edges in (False, True):
            arrive(-1, edges)
            convolve(2, not edges, False, True)

    @pl.when(above)
    def _():
        def go(b, carry):
            low_copy(b).wait_send()
            return carry

        lax.fori_loop(0, bands, go, 0)
    for h in range(2):
        for u in range(2):
            for v in range(2):
                for slot in range(3):
                    stage(slot, h, u, v).wait_send()
    for ds in (1, -1):
        @pl.when(there(ds))
        def _(ds=ds):
            for h in range(2):
                for u in range(2):
                    for v in range(2):
                        halo_copy(ds, h, u, v).wait_send()
            for dc in (1, -1):
                @pl.when(beside(-dc))
                def _(dc=dc):
                    pass_copy(ds, dc).wait_send()
    for dc in (1, -1):
        @pl.when(beside(dc))
        def _(dc=dc):
            row_copy(dc).wait_send()


def save(a_ref, b_ref, to_a, to_b, sems):
    one, two = pltpu.make_async_copy(a_ref, to_a, sems.at[0]), pltpu.make_async_copy(b_ref, to_b, sems.at[1])
    one.start()
    two.start()
    one.wait()
    two.wait()


def local_square(volume, weight_one, bias_one, weight_two, bias_two):
    c, planes, height, width = volume.shape
    k = weight_one.shape[4]
    parts, slabs = lax.axis_size("chan"), lax.axis_size("slab")
    deep = 256 // c
    bands = height // deep
    rows, cols = height // 2, width // 2
    mine = rows // parts
    hbm = pl.BlockSpec(memory_space=pltpu.HBM)
    near = pl.BlockSpec(memory_space=pl.ANY)
    vmem = pl.BlockSpec(memory_space=pltpu.VMEM)
    dma = pltpu.SemaphoreType.DMA
    block = jax.ShapeDtypeStruct((mine, cols, k), BF)
    act, grouped = pl.pallas_call(
        functools.partial(square, slabs),
        out_shape=(pltpu.VMEM((mine, cols, k), BF),) * 2,
        in_specs=[hbm] * 5,
        out_specs=(vmem, vmem),
        scratch_shapes=[
            pltpu.VMEM((planes, c, bands, deep, width), BF),
            pltpu.VMEM(weight_one.shape, BF), pltpu.VMEM(weight_two.shape, BF),
            pltpu.VMEM((1, k), F32), pltpu.VMEM((1, k), F32),
            pltpu.VMEM((c, bands, deep, width), BF),
            pltpu.VMEM((9, height * c // 128 + 1, cols, 128), BF),
            pltpu.VMEM((rows, cols, k), BF),
            pltpu.VMEM((parts - 1, mine, cols, k), BF),
            pltpu.VMEM((3, mine + 2, cols, k), BF),
            pltpu.VMEM((9 * 256, k), BF),
            pltpu.VMEM((9 * 128, k), BF),
            pltpu.VMEM((3, 9 * k, k), BF),
            pltpu.VMEM((2, mine // 2 * cols, k), F32),
            dma((2,)), dma((4,)),
            dma((bands,)), dma((bands,)),
            dma((3, 2, 2, 2)), dma((3, 2, 2, 2)),
            dma((2, 2, 2, 2)), dma((2, 2, 2, 2)),
            dma((2,)), dma((2,)),
            dma((2, 2)), dma((2, 2)),
        ],
        compiler_params=pltpu.CompilerParams(vmem_limit_bytes=58 << 20, collective_id=0, has_side_effects=True),
    )(volume.reshape(c, planes, bands, deep, width), weight_one, bias_one.reshape(1, k), weight_two, bias_two.reshape(1, k))
    act, grouped = pl.pallas_call(
        save, out_shape=(block, block), in_specs=[near, near], out_specs=(hbm, hbm), scratch_shapes=[dma((2,))],
        compiler_params=pltpu.CompilerParams(vmem_limit_bytes=1 << 20),
    )(act, grouped)
    return act[None], grouped[None]


def body(parts, slabs, own_ref, k1_ref, b1_ref, k2_ref, b2_ref, act_ref, out_ref,
         low_ref, t_ref, part_ref, recv_ref, a_ref, w1_ref, w2_ref, acc_ref,
         low_send, low_recv, sum_send, sum_recv, halo_send, halo_recv):
    c = own_ref.shape[2]
    tall = 128 // c
    wins = own_ref.shape[1] // tall
    half = own_ref.shape[3] // 2
    mine, q, k = act_ref.shape
    outs = tall // 2
    step = 4 * outs if mine % (4 * outs) == 0 else mine
    pieces = mine // step
    me, slab = lax.axis_index("chan"), lax.axis_index("slab")

    def peer(s):
        if parts == 4:
            return 2 * lax.rem(me // 2 + lax.div(s, 2), 2) + lax.rem(lax.rem(me, 2) + lax.rem(s, 2), 2)
        return lax.rem(me + s, parts)

    def inside(dc, ds):
        ok = None
        for coord, move, size in ((me, dc, parts), (slab, ds, slabs)):
            if move:
                one = coord + move < size if move > 0 else coord + move >= 0
                ok = one if ok is None else jnp.logical_and(ok, one)
        return ok

    barrier = pltpu.get_barrier_semaphore()
    for s in range(1, parts):
        pl.semaphore_signal(barrier, inc=1, device_id={"chan": peer(jnp.int32(s)), "slab": slab}, device_id_type=MESH)
    for dc, ds in AROUND:
        if ds:
            @pl.when(inside(dc, ds))
            def _(dc=dc, ds=ds):
                pl.semaphore_signal(barrier, inc=1, device_id={"chan": me + dc, "slab": slab + ds}, device_id_type=MESH)
    one = jnp.int32(1)
    across = jnp.minimum(slab, one) + jnp.minimum(jnp.int32(slabs - 1) - slab, one)
    along = one + jnp.minimum(me, one) + jnp.minimum(jnp.int32(parts - 1) - me, one)
    pl.semaphore_wait(barrier, jnp.int32(parts - 1) + across * along)

    def low_copy():
        return pltpu.make_async_remote_copy(
            src_ref=own_ref.at[own_ref.shape[0] - 1], dst_ref=low_ref, send_sem=low_send, recv_sem=low_recv,
            device_id={"chan": me, "slab": slab + 1}, device_id_type=MESH)

    @pl.when(slab + 1 < slabs)
    def _():
        low_copy().start()

    w1_ref[...] = jnp.zeros_like(w1_ref)
    for e in range(9):
        i, l = divmod(e, 3)
        for par in range(outs):
            for j in range(3):
                start = e * 256 + (tall - 1 + 2 * par + j) * c
                w1_ref[start:start + c, par * k:(par + 1) * k] = k1_ref[i, j, l]
    m = k2_ref.shape[3]
    group = lax.broadcasted_iota(jnp.int32, (m, k), 1) // m
    for i in range(3):
        for l in range(3):
            for j in range(3):
                taps = k2_ref[i, j, l]
                for g in range(k // m):
                    w2_ref[i, l, j * k + g * m:j * k + (g + 1) * m] = jnp.where(group == g, taps, jnp.zeros_like(taps))
    width = own_ref.shape[3]
    spot = lax.broadcasted_iota(jnp.int32, (half, width), 1) - 2 * lax.broadcasted_iota(jnp.int32, (half, width), 0)
    sel = jnp.concatenate([jnp.where(spot == l - 1, 1.0, 0.0) for l in range(3)], axis=0).astype(BF)
    for e in range(9):
        t_ref[e, 0] = jnp.zeros_like(t_ref[e, 0])

    def decimate(d):
        def go(b, carry):
            rows = pl.ds(4 * tall * b, 4 * tall)
            x = low_ref[rows] if d == 0 else own_ref[d - 1, rows]
            x = x.reshape(512, own_ref.shape[3])
            t = lax.dot_general(sel, x, (((1,), (1,)), ((), ())), preferred_element_type=F32).astype(BF)
            for l in range(3):
                for u in range(4):
                    t_ref[3 * d + l, 4 * b + u + 1] = t[l * half:(l + 1) * half, 128 * u:128 * (u + 1)]
            return carry

        lax.fori_loop(0, wins // 4, go, 0)

    decimate(1)
    decimate(2)

    @pl.when(slab == 0)
    def _():
        low_ref[...] = jnp.zeros_like(low_ref)

    @pl.when(slab > 0)
    def _():
        low_copy().wait_recv()

    decimate(0)

    def chunk(b):
        lhs = []
        for e in range(9):
            lhs.append(t_ref[e, pl.ds(4 * b, 4)].reshape(4 * half, 128))
            lhs.append(t_ref[e, pl.ds(4 * b + 1, 4)].reshape(4 * half, 128))
        res = jnp.dot(jnp.concatenate(lhs, axis=1), w1_ref[...], preferred_element_type=F32).astype(BF)
        for u in range(4):
            for par in range(outs):
                part_ref[4 * outs * b + outs * u + par] = res[u * half:(u + 1) * half, par * k:(par + 1) * k]

    def sum_copy(s, h):
        to = peer(s)
        return pltpu.make_async_remote_copy(
            src_ref=part_ref.at[pl.ds(to * mine + h * step, step)], dst_ref=recv_ref.at[s - 1, pl.ds(h * step, step)],
            send_sem=sum_send.at[s - 1, h], recv_sem=sum_recv.at[s - 1, h],
            device_id={"chan": to, "slab": slab}, device_id_type=MESH)

    paired = parts == 4 and step == 4 * outs
    hop = step // 2

    def stage(slot, h, u):
        to = peer(jnp.int32(1 + u if slot < 2 else 2 - u))
        block = peer(jnp.int32(3)) if slot == 1 else to
        at = h * step + u * hop
        return pltpu.make_async_remote_copy(
            src_ref=part_ref.at[pl.ds(block * mine + at, hop)], dst_ref=recv_ref.at[slot, pl.ds(at, hop)],
            send_sem=sum_send.at[slot, 2 * h + u], recv_sem=sum_recv.at[slot, 2 * h + u],
            device_id={"chan": to, "slab": slab}, device_id_type=MESH)

    if paired:
        far, across_x, across_y = (peer(jnp.int32(s)) for s in (3, 1, 2))

        def first(h, carry):
            chunk(far * pieces + h)
            stage(1, h, 0).start()
            stage(1, h, 1).start()
            chunk(across_x * pieces + h)
            stage(0, h, 0).start()
            chunk(across_y * pieces + h)
            stage(0, h, 1).start()
            return carry

        lax.fori_loop(0, pieces, first, 0)
        for h in range(pieces):
            for u, block in ((0, across_y), (1, across_x)):
                at = h * step + u * hop
                stage(1, h, u).wait_recv()
                here = pl.ds(block * mine + at, hop)
                both = part_ref[here].astype(F32) + recv_ref[1, at:at + hop].astype(F32)
                part_ref[here] = both.astype(BF)
                stage(2, h, u).start()
            chunk(me * pieces + h)
    elif step == 4 * outs:
        def away(n, carry):
            s, h = parts - 1 - lax.rem(n, parts - 1), lax.div(n, parts - 1)
            chunk(peer(s) * pieces + h)
            sum_copy(s, h).start()
            return carry

        def home(h, carry):
            chunk(me * pieces + h)
            return carry

        lax.fori_loop(0, (parts - 1) * pieces, away, 0)
        lax.fori_loop(0, pieces, home, 0)
    else:
        def one(n, carry):
            chunk(n)
            return carry

        lax.fori_loop(0, wins // 4, one, 0)
        for s in range(1, parts):
            sum_copy(jnp.int32(s), 0).start()

    def spots(dc, ds, h):
        if dc == 0:
            rows = pl.ds(1 + h * step, step)
            return a_ref.at[1, rows], a_ref.at[1 - ds, rows]
        return a_ref.at[1, pl.ds(mine if dc > 0 else 1, 1)], a_ref.at[1 - ds, pl.ds(0 if dc > 0 else mine + 1, 1)]

    def halo_copy(n, h):
        dc, ds = AROUND[n]
        src, dst = spots(dc, ds, h)
        return pltpu.make_async_remote_copy(
            src_ref=src, dst_ref=dst, send_sem=halo_send.at[n, h], recv_sem=halo_recv.at[n, h],
            device_id={"chan": me + dc, "slab": slab + ds}, device_id_type=MESH)

    def due(dc):
        return range(pieces) if dc == 0 else (pieces - 1,) if dc > 0 else (0,)

    def arrive(n):
        dc, ds = AROUND[n]
        there = inside(-dc, -ds)
        for h in due(dc):
            @pl.when(there)
            def _(h=h):
                halo_copy(n, h).wait_recv()

            @pl.when(jnp.logical_not(there))
            def _(h=h):
                dst = spots(dc, ds, h)[1]
                dst[...] = jnp.zeros(dst.shape, BF)

    for h in range(pieces):
        for slot in (0, 2) if paired else ():
            stage(slot, h, 0).wait_recv()
            stage(slot, h, 1).wait_recv()
        for s in () if paired else range(1, parts):
            sum_copy(jnp.int32(s), h).wait_recv()
        for r in range(h * step, (h + 1) * step, 4):
            total = part_ref[pl.ds(me * mine + r, 4)].astype(F32)
            for slot in (0, 2) if paired else range(parts - 1):
                total += recv_ref[slot, r:r + 4].astype(F32)
            act = leaky(total + b1_ref[...]).astype(BF)
            act_ref[r:r + 4] = act
            a_ref[1, r + 1:r + 5] = act
        for n, (dc, ds) in enumerate(AROUND):
            if h in due(dc):
                @pl.when(inside(dc, ds))
                def _(n=n, h=h):
                    halo_copy(n, h).start()

    for i, last in ((1, False), (0, False), (2, True)):
        for n, (dc, ds) in enumerate(AROUND):
            if 1 - ds == i:
                arrive(n)

        def rows4(b, carry, i=i, last=last):
            lhs = jnp.concatenate([a_ref[i, pl.ds(4 * b + j, 4)].reshape(4 * q, k) for j in range(3)], axis=1)
            here = pl.ds(4 * q * b, 4 * q)
            accs = []
            for l in range(3):
                acc = jnp.dot(lhs, w2_ref[i, l], preferred_element_type=F32)
                if i != 1:
                    acc += acc_ref[l, here]
                accs.append(acc)
            if not last:
                for l in range(3):
                    acc_ref[l, here] = accs[l]
                return carry
            col = lax.rem(lax.broadcasted_iota(jnp.int32, (4 * q, k), 0), q)
            left = jnp.where(col == 0, 0.0, pltpu.roll(accs[0], 1, 0))
            right = jnp.where(col == q - 1, 0.0, pltpu.roll(accs[2], 4 * q - 1, 0))
            res = left + accs[1] + right + b2_ref[...]
            out_ref[pl.ds(4 * b, 4)] = res.reshape(4, q, k).astype(BF)
            return carry

        lax.fori_loop(0, mine // 4, rows4, 0)

    @pl.when(slab + 1 < slabs)
    def _():
        low_copy().wait_send()
    for s in range(1, parts):
        for h in range(pieces):
            if paired:
                stage(s - 1, h, 0).wait_send()
                stage(s - 1, h, 1).wait_send()
            else:
                sum_copy(jnp.int32(s), h).wait_send()
    for n, (dc, ds) in enumerate(AROUND):
        for h in due(dc):
            @pl.when(inside(dc, ds))
            def _(n=n, h=h):
                halo_copy(n, h).wait_send()


def local(volume, weight_one, bias_one, weight_two, bias_two):
    c, planes, height, width = volume.shape
    k = weight_one.shape[4]
    parts, slabs = lax.axis_size("chan"), lax.axis_size("slab")
    own_t = volume.transpose(1, 2, 0, 3)
    rows, cols = height // 2, width // 2
    mine = rows // parts
    step = 256 // c if mine % (256 // c) == 0 else mine
    vmem = pl.BlockSpec(memory_space=pltpu.VMEM)
    dma = pltpu.SemaphoreType.DMA
    block = jax.ShapeDtypeStruct((mine, cols, k), BF)
    act, grouped = pl.pallas_call(
        functools.partial(body, parts, slabs),
        out_shape=(block, block),
        in_specs=[vmem] * 5,
        out_specs=(vmem, vmem),
        scratch_shapes=[
            pltpu.VMEM((height, c, width), BF),
            pltpu.VMEM((9, height * c // 128 + 1, cols, 128), BF),
            pltpu.VMEM((rows, cols, k), BF),
            pltpu.VMEM((parts - 1, mine, cols, k), BF),
            pltpu.VMEM((3, mine + 2, cols, k), BF),
            pltpu.VMEM((9 * 256, 64 // c * k), BF),
            pltpu.VMEM((3, 3, 3 * k, k), BF),
            pltpu.VMEM((3, mine * cols, k), F32),
            dma, dma,
            dma((parts - 1, 2 * mine // step)), dma((parts - 1, 2 * mine // step)),
            dma((8, mine // step)), dma((8, mine // step)),
        ],
        compiler_params=pltpu.CompilerParams(vmem_limit_bytes=48 << 20, collective_id=0, has_side_effects=True),
    )(own_t, weight_one, bias_one.reshape(1, k), weight_two, bias_two.reshape(1, k))
    return act[None], grouped[None]


def solution(mesh):
    in_specs = (P("chan", "slab", None, None), P(None, None, None, "chan", None), P(), P(), P())
    out_specs = (P("slab", "chan", None, None), P("slab", "chan", None, None))
    run = local_square if mesh.shape["chan"] == 4 else local
    return jax.shard_map(run, mesh=mesh, in_specs=in_specs, out_specs=out_specs, check_vma=False)
```
